32 devices in a mesh: req: 4 (over x, core), mlp: 8 (over z, y).
Axes of the slice: x: 2, y: 2, z: 4, core: 2. Of those that a mesh axis runs over, the one named last changes fastest.
Arguments:
- resid: bfloat16 [4096, 3072], P(('req', 'mlp')), may hold values from -6 to 6
- queries: bfloat16 [4096, 1536], P(('req', 'mlp')), may hold values from -240 to 240
- fresh_keys: bfloat16 [4096, 256], P(('req', 'mlp')), may hold values from -6 to 6
- fresh_values: bfloat16 [4096, 256], P(('req', 'mlp')), may hold values from -6 to 6
- paged_key_cache: bfloat16 [64, 128, 256], P(('req', 'mlp')), may hold values from -6 to 6
- paged_value_cache: bfloat16 [64, 128, 256], P(('req', 'mlp')), may hold values from -6 to 6
- page_table: int32 [4, 16], P('req'), may hold values from 0 to 15, as said below
- cache_lengths: int32 [4], P('req'), may hold values from 1 to 2048, as said below
- out_weight: bfloat16 [1536, 3072], replicated, may hold values from -0.15625 to 0.15625
- norm_gain: float32 [3072], replicated, may hold values from 0.5 to 1.5
- gate_weight: bfloat16 [3072, 8192], P('req', 'mlp'), may hold values from -0.109375 to 0.109375
- up_weight: bfloat16 [3072, 8192], P('req', 'mlp'), may hold values from -0.109375 to 0.109375
- down_weight: bfloat16 [8192, 3072], P('mlp', 'req'), may hold values from -0.0625 to 0.0625
Outputs:
- layer_out: bfloat16 [4096, 3072], P(('req', 'mlp'))
The draws below stay inside these ranges and needn't reach their ends.
Inputs may be any that keep to these rules, and one draw needn't show every extreme that they name: `page_table`: within the 1 request of one index of req the entries are a permutation of 0 to 15. `cache_lengths`: half of the requests hold at most 128 cached tokens, the other half more than 1920; some request holds exactly 2048.
All inputs are finite; a program needn't handle non-finite values.
Results may differ from the reference program's by a relative error of at most 0.0085.
Values may be sent and summed in bfloat16 or wider, within the bound.
A program may use at most 128 MiB of HBM per device.

```python
import jax
import jax.numpy as jnp
from jax import lax

D = 3072
QUERY_HEADS = 12
KEY_VALUE_HEADS = 2
HEAD_SIZE = 128
FF = 8192
REQ_DEV = 1
PAGE_TOKENS = 128
PAGES = 16
NEW_TOKENS = 1024
REQUEST_COUNT = 4
TOKEN_COUNT = 4096
CONTEXT_LIMIT = 2048
GROUP_SLOTS = 16
POOL_PAGES = 64
N_MLP = 8


def draw_queries(key, part):
    base = jnp.clip(jax.random.normal(key, (TOKEN_COUNT, QUERY_HEADS * HEAD_SIZE), jnp.float32), -6.0, 6.0)
    return base.astype(jnp.bfloat16)


def draw_page_table(key, part):
    blocks = REQUEST_COUNT // REQ_DEV
    joined_keys = jax.random.split(jax.random.fold_in(key, 11), blocks)
    orders = jax.vmap(lambda k: jax.random.permutation(k, GROUP_SLOTS))(joined_keys)
    return orders.reshape(REQUEST_COUNT, PAGES).astype(jnp.int32)


def draw_cache_lengths(key, part):
    order = jax.random.permutation(jax.random.fold_in(key, 21), REQUEST_COUNT).astype(jnp.int32)
    longer = CONTEXT_LIMIT - jax.random.randint(jax.random.fold_in(key, 22), (REQUEST_COUNT,), 0, PAGE_TOKENS)
    shorter = jax.random.randint(jax.random.fold_in(key, 23), (REQUEST_COUNT,), 1, PAGE_TOKENS + 1)
    lengths = jnp.where(order < REQUEST_COUNT // 2, longer, shorter)
    lengths = jnp.where(order == 0, CONTEXT_LIMIT, lengths)
    return lengths.astype(jnp.int32)


def shard_levels(key, extent, cuts, least, high):
    def one(position, parts):
        heights = jax.random.uniform(jax.random.fold_in(jax.random.fold_in(key, 6), position), (parts,), jnp.float32, least / len(cuts), high / len(cuts))
        return jnp.repeat(jnp.exp(heights), extent[position] // parts).reshape((-1,) + (1,) * (len(extent) - position - 1))

    gain = one(*cuts[0])
    for cut in cuts[1:]:
        gain = gain * one(*cut)
    return gain


def noise(key, shape, scale, most, cuts=(), kind=jnp.bfloat16):
    factor_of = shard_levels(key, shape, cuts, -0.22, 0.18) if cuts else 1.0
    entries = jax.random.normal(key, shape, jnp.float32) * scale * factor_of
    return jnp.minimum(jnp.maximum(entries, -most), most).astype(kind)


def setup_inputs(seed: int = 0) -> dict:
    seeds = jax.random.split(jax.random.key(seed), 14)
    resid = noise(seeds[0], (TOKEN_COUNT, D), 1.0, 6.0, ((0, 32),))
    queries = draw_queries(jax.random.fold_in(seeds[13], 71), 0)
    fresh_keys = noise(seeds[2], (TOKEN_COUNT, KEY_VALUE_HEADS * HEAD_SIZE), 1.0, 6.0, ((0, 32),))
    fresh_values = noise(seeds[3], (TOKEN_COUNT, KEY_VALUE_HEADS * HEAD_SIZE), 1.0, 6.0, ((0, 32),))
    paged_key_cache = noise(seeds[4], (POOL_PAGES, PAGE_TOKENS, KEY_VALUE_HEADS * HEAD_SIZE), 1.0, 6.0, ((0, 32),))
    paged_value_cache = noise(seeds[5], (POOL_PAGES, PAGE_TOKENS, KEY_VALUE_HEADS * HEAD_SIZE), 1.0, 6.0, ((0, 32),))
    page_table = draw_page_table(jax.random.fold_in(seeds[13], 71), 0)
    cache_lengths = draw_cache_lengths(jax.random.fold_in(seeds[13], 71), 0)
    out_weight = noise(seeds[8], (QUERY_HEADS * HEAD_SIZE, D), (QUERY_HEADS * HEAD_SIZE) ** -0.5, 0.15625)
    norm_gain = jnp.clip(1.0 + 0.1 * jax.random.normal(seeds[9], (D,), jnp.float32), 0.5, 1.5)
    gate_weight = noise(seeds[10], (D, FF), D ** -0.5, 0.109375, ((0, 4), (1, 8)))
    up_weight = noise(seeds[11], (D, FF), D ** -0.5, 0.109375, ((0, 4), (1, 8)))
    down_weight = noise(seeds[12], (FF, D), FF ** -0.5, 0.0625, ((0, 8), (1, 4)))
    return {"resid": resid, "queries": queries, "fresh_keys": fresh_keys, "fresh_values": fresh_values, "paged_key_cache": paged_key_cache, "paged_value_cache": paged_value_cache, "page_table": page_table, "cache_lengths": cache_lengths, "out_weight": out_weight, "norm_gain": norm_gain, "gate_weight": gate_weight, "up_weight": up_weight, "down_weight": down_weight}


def attend_request(rows_of_queries, rows_of_keys, rows_of_values, table_row, length, request, paged_key_cache, paged_value_cache):
    group_ratio = QUERY_HEADS // KEY_VALUE_HEADS
    block = request // REQ_DEV
    cache_positions = (table_row + block * GROUP_SLOTS).astype(jnp.int32)
    stored_keys = jnp.take(paged_key_cache, cache_positions, axis=0).reshape(CONTEXT_LIMIT, KEY_VALUE_HEADS * HEAD_SIZE)
    stored_values = jnp.take(paged_value_cache, cache_positions, axis=0).reshape(CONTEXT_LIMIT, KEY_VALUE_HEADS * HEAD_SIZE)
    joined_keys = jnp.concatenate([stored_keys, rows_of_keys], axis=0).astype(jnp.float32).reshape(CONTEXT_LIMIT + NEW_TOKENS, KEY_VALUE_HEADS, HEAD_SIZE)
    joined_values = jnp.concatenate([stored_values, rows_of_values], axis=0).astype(jnp.float32).reshape(CONTEXT_LIMIT + NEW_TOKENS, KEY_VALUE_HEADS, HEAD_SIZE)
    heads_of_queries = rows_of_queries.astype(jnp.float32).reshape(NEW_TOKENS, KEY_VALUE_HEADS, group_ratio, HEAD_SIZE)
    scores = jnp.einsum('tgrd,kgd->grtk', heads_of_queries, joined_keys) * HEAD_SIZE ** (-0.5)
    columns = jnp.arange(CONTEXT_LIMIT + NEW_TOKENS, dtype=jnp.int32)
    rows = jnp.arange(NEW_TOKENS, dtype=jnp.int32)
    mask = jnp.where(columns[None, :] < CONTEXT_LIMIT, (columns < length)[None, :], columns[None, :] - CONTEXT_LIMIT <= rows[:, None])
    scores = jnp.where(mask, scores, -1e+30)
    peak = lax.optimization_barrier(jnp.max(scores, axis=-1, keepdims=True))
    expo = jnp.where(mask, jnp.exp(scores - peak), 0.0)
    total = lax.optimization_barrier(jnp.sum(expo, axis=-1))
    rounded = lax.optimization_barrier(expo.astype(jnp.bfloat16)).astype(jnp.float32)
    summed = jnp.einsum('grtk,kgd->grtd', rounded, joined_values) / total[..., None]
    return jnp.transpose(summed, (2, 0, 1, 3)).reshape(NEW_TOKENS, QUERY_HEADS * HEAD_SIZE).astype(jnp.bfloat16)

def reference(resid, queries, fresh_keys, fresh_values, paged_key_cache, paged_value_cache, page_table, cache_lengths, out_weight, norm_gain, gate_weight, up_weight, down_weight):
    query_sets = queries.reshape(REQUEST_COUNT, NEW_TOKENS, QUERY_HEADS * HEAD_SIZE)
    grouped_keys = fresh_keys.reshape(REQUEST_COUNT, NEW_TOKENS, KEY_VALUE_HEADS * HEAD_SIZE)
    grouped_values = fresh_values.reshape(REQUEST_COUNT, NEW_TOKENS, KEY_VALUE_HEADS * HEAD_SIZE)
    numbers = jnp.arange(REQUEST_COUNT, dtype=jnp.int32)

    def one(items):
        return attend_request(items[0], items[1], items[2], items[3], items[4], items[5], paged_key_cache, paged_value_cache)
    attn = lax.map(one, (query_sets, grouped_keys, grouped_values, page_table, cache_lengths, numbers)).reshape(TOKEN_COUNT, QUERY_HEADS * HEAD_SIZE)
    h = resid.astype(jnp.float32) + jnp.dot(attn, out_weight, preferred_element_type=jnp.float32)
    normed = (h * lax.rsqrt(lax.optimization_barrier(jnp.mean(h * h, axis=-1, keepdims=True)) + 1e-05) * norm_gain).astype(jnp.bfloat16)
    width_block = FF // N_MLP

    def add_block(index, total):
        start = index * width_block
        gate = jnp.dot(normed, lax.dynamic_slice_in_dim(gate_weight, start, width_block, 1), preferred_element_type=jnp.float32)
        upper = jnp.dot(normed, lax.dynamic_slice_in_dim(up_weight, start, width_block, 1), preferred_element_type=jnp.float32)
        hidden = (jax.nn.silu(gate) * upper).astype(jnp.bfloat16)
        partial_value = jnp.dot(hidden, lax.dynamic_slice_in_dim(down_weight, start, width_block, 0), preferred_element_type=jnp.float32)
        return total + lax.optimization_barrier(partial_value.astype(jnp.bfloat16)).astype(jnp.float32)
    summed = lax.fori_loop(0, N_MLP, add_block, jnp.zeros((TOKEN_COUNT, D), jnp.float32))
    return (h + summed).astype(jnp.bfloat16)
```

```python
import functools
import math

import jax
import jax.numpy as jnp
from jax import lax
from jax.experimental import pallas as pl
from jax.experimental.pallas import tpu as pltpu
from jax.sharding import PartitionSpec as P

QUERY_HEADS = 12
KEY_VALUE_HEADS = 2
HEAD_SIZE = 128
GROUP = QUERY_HEADS // KEY_VALUE_HEADS
KV_COLS = KEY_VALUE_HEADS * HEAD_SIZE
ATTN = QUERY_HEADS * HEAD_SIZE
MESH = pl.DeviceIdType.MESH


def flip(a, k):
    bit = 1
    while bit <= k:
        if k & bit:
            a = a + bit - 2 * bit * (lax.rem(a // bit, 2))
        bit *= 2
    return a


def at_least(u, v):
    return (u - v + 1024) // 1024


def nearest(a, count, j):
    if j == 0:
        return a
    low = 1 - at_least(a, count // 2)
    room = low * a + (1 - low) * (count - 1 - a)
    both = at_least(2 * room, j)
    step = (j + 1) // 2
    return a + both * (-step if j % 2 else step) + (1 - both) * (2 * low - 1) * (j - room)


def kernel(
    n, nr,
    table, length, q_ref, resid_ref, gain_ref, fk, fv, pk, pv, ow, wg, wu, wd,
    out_ref,
    kb, vb, nrm, wgs, wus, wds, big, yr, zr, h, attn, top, den, bias, hid,
    loc, ss, kv_recv, n_recv, w_recv, d_recv, y_recv, z_recv,
):
    A, X = n // 2, nr // 2
    me, r = lax.axis_index("mlp"), lax.axis_index("req")
    a, b = me // 2, lax.rem(me, 2)
    x, c = r // 2, lax.rem(r, 2)
    partner, sibling = a * 2 + 1 - b, x * 2 + 1 - c
    mate = a + 1 - 2 * lax.rem(a, 2)
    has_l, has_r = a > 0, a < A - 1
    T, D = resid_ref.shape
    T2 = T // 2
    own_pages, page_tokens = pk.shape[:2]
    cached = own_pages * page_tokens
    R = cached + T
    depth, F = wg.shape
    Dq = wd.shape[1]
    bf16, f32 = jnp.bfloat16, jnp.float32

    def rpeer(k):
        return flip(x, k) * 2 + c

    def remote(src, dst, sem, recv_sem, axis, idx):
        return pltpu.make_async_remote_copy(
            src_ref=src, dst_ref=dst, send_sem=sem, recv_sem=recv_sem,
            device_id={axis: idx}, device_id_type=MESH,
        )

    started = []

    def send(src, dst, recv_sem, axis, idx, when=None):
        copy = remote(src, dst, ss.at[len(started)], recv_sem, axis, idx)
        started.append((copy, when))
        if when is None:
            copy.start()
        else:
            pl.when(when)(copy.start)

    def arrive(ref, recv_sem, when=None):
        copy = remote(ref, ref, recv_sem, recv_sem, "mlp", partner)
        if when is None:
            copy.wait_recv()
        else:
            pl.when(when)(copy.wait_recv)

    base = pl.multiple_of(me * R, 128)
    mine = []
    for i, (buf, pages, fresh) in enumerate(((kb, pk, fk), (vb, pv, fv))):
        for j in range(own_pages):
            mine.append(pltpu.make_async_copy(
                pages.at[j], buf.at[pl.ds(base + j * page_tokens, page_tokens), :], loc.at[i, j]))
        mine.append(pltpu.make_async_copy(fresh, buf.at[pl.ds(base + cached, T), :], loc.at[i, own_pages]))
    for copy in mine:
        copy.start()

    def w_slot(i, s):
        if i == 2:
            return wds.at[s]
        buf = wgs if i == 0 else wus
        return buf.at[pl.ds(pl.multiple_of(s * depth, 128), depth), :]

    weights = (wg, wu, wd)
    own_w = [pltpu.make_async_copy(weights[i], w_slot(i, r), loc.at[2, i]) for i in range(3)]
    own_ow = pltpu.make_async_copy(ow, big.at[pl.ds(0, ATTN), :], loc.at[3, 0])

    barrier = pltpu.get_barrier_semaphore()

    def greet(axis, idx):
        pl.semaphore_signal(barrier, inc=1, device_id={axis: idx}, device_id_type=MESH)

    greet("mlp", partner)
    greet("req", sibling)
    for k in range(1, X):
        greet("req", rpeer(k))
    pl.when(has_l)(lambda: greet("mlp", me - 2))
    pl.when(has_r)(lambda: greet("mlp", me + 2))
    pl.semaphore_wait(barrier, X + 1 + has_l.astype(jnp.int32) + has_r.astype(jnp.int32))

    def kv_slot(part):
        buf = (kb, vb)[part]
        return lambda s: buf.at[pl.ds(pl.multiple_of(s * R, 128), R), :], lambda s: kv_recv.at[part, s]

    half = D // 2

    def n_rows(hh, s):
        return pl.ds(pl.multiple_of((hh * n + s) * T2, T2), T2)

    def n_slot(hh, f):
        return (
            lambda s: nrm.at[n_rows(hh, s), pl.ds(f * half, half)],
            lambda s: n_recv.at[hh * 2 + f, s],
        )

    def spread(kind):
        slot, sem = kind
        send(slot(me), slot(me), sem(me), "mlp", me + 2, has_r)
        send(slot(me), slot(me), sem(me), "mlp", me - 2, has_l)
        send(slot(me), slot(me), sem(me), "mlp", partner)

    def forward(kind, k, mated):
        slot, sem = kind
        pos = nearest(a, A, k)
        s = pos * 2 + b
        arrive(slot(s), sem(s))
        right = at_least(a, pos)
        to = a + 2 * right - 1
        send(slot(s), slot(s), sem(s), "mlp", to * 2 + b, (to >= 0) & (to < A))
        send(slot(s), slot(s), sem(s), "mlp", partner, (pos != mate) if mated else None)

    def hop(kind):
        slot, sem = kind
        arrive(slot(partner), sem(partner))
        send(slot(partner), slot(partner), sem(partner), "mlp", mate * 2 + b)

    def other(kind, k):
        slot, sem = kind
        s = nearest(a, A, k) * 2 + 1 - b
        arrive(slot(s), sem(s))

    kv = [kv_slot(0), kv_slot(1)]
    for part in range(2):
        for copy in mine[part * (own_pages + 1) : (part + 1) * (own_pages + 1)]:
            copy.wait()
        spread(kv[part])
    for i in range(2):
        for k in range(1, X):
            send(weights[i], w_slot(i, r), w_recv.at[i, r], "req", rpeer(k))
    own_w[2].start()
    send(wd, w_slot(2, r), w_recv.at[2, r], "req", sibling)
    own_ow.start()
    for i in range(2):
        own_w[i].start()
        send(weights[i], w_slot(i, r), w_recv.at[i, r], "req", sibling)

    factor = HEAD_SIZE ** (-0.5) * math.log2(math.e)
    ahead = lax.broadcasted_iota(jnp.int32, (T, T), 1) - lax.broadcasted_iota(jnp.int32, (T, T), 0)
    lane = lax.broadcasted_iota(jnp.int32, (T, page_tokens), 1)

    def mask(k):
        for j in range(2):
            s = nearest(a, A, k) * 2 + j
            for p in range(own_pages):
                page = jnp.int32(0)
                for i in range(table.shape[1]):
                    page = page + jnp.where(table[0, i] == s * own_pages + p, i, 0)
                live = lane < length[0] - page * page_tokens
                bias[:, j * R + p * page_tokens : j * R + (p + 1) * page_tokens] = jnp.where(live, 0.0, -1e30)
            bias[:, j * R + cached : (j + 1) * R] = jnp.where(ahead <= (me - s) * T, 0.0, -1e30)

    def attend(k, first, last):
        rows = pl.ds(pl.multiple_of(nearest(a, A, k) * 2 * R, 128), 2 * R)

        def step(i, carry):
            head = 2 * i
            g = head // GROUP
            c0 = pl.ds(pl.multiple_of(head * HEAD_SIZE, 128), HEAD_SIZE)
            c1 = pl.ds(pl.multiple_of(head * HEAD_SIZE + HEAD_SIZE, 128), HEAD_SIZE)
            gc = pl.ds(pl.multiple_of(g * HEAD_SIZE, 128), HEAD_SIZE)
            qq = jnp.concatenate([q_ref[:, c0], q_ref[:, c1]], axis=0)
            s = lax.dot_general(
                qq, kb[rows, gc], (((1,), (1,)), ((), ())), preferred_element_type=f32
            )
            s = ((s * factor).reshape(2, T, 2 * R) + bias[...][None]).reshape(2 * T, 2 * R)
            most = jnp.max(s, axis=-1, keepdims=True)
            if not first:
                before = top[i]
                most = jnp.maximum(most, before)
                scale = jnp.exp2(before - most)
            e = jnp.exp2(s - most)
            total = jnp.sum(e, axis=-1, keepdims=True)
            o = jnp.dot(e.astype(bf16), vb[rows, gc], preferred_element_type=f32)
            if not first:
                total = total + den[i] * scale
                o = o + jnp.concatenate([h[:, c0], h[:, c1]], axis=0) * scale
            if last:
                o = o / total
                attn[:, c0] = o[:T].astype(bf16)
                attn[:, c1] = o[T:].astype(bf16)
            else:
                top[i] = most
                den[i] = total
                h[:, c0] = o[:T]
                h[:, c1] = o[T:]
            return carry

        lax.fori_loop(0, QUERY_HEADS // 2, step, 0)

    def both(f, *args):
        for part in range(2):
            f(kv[part], *args)

    mask(0)
    both(other, 0)
    attend(0, True, A == 1)
    fh = F // 2
    own_w[2].wait()
    arrive(w_slot(2, sibling), w_recv.at[2, sibling])

    def d_part(s, part):
        return wds.at[s, pl.ds(pl.multiple_of(part * fh, 16), fh), :]

    for cc in range(2):
        for k in range(1, X):
            s = x * 2 + cc
            send(d_part(s, c), d_part(s, c), d_recv.at[s, c], "req", rpeer(k))
    for k in range(1, A):
        both(forward, k, False)
        mask(k)
        if k < A - 1:
            both(other, k)
            attend(k, False, False)
    if A > 1:
        both(other, A - 1)
        attend(A - 1, False, True)

    own_ow.wait()

    def project(j, squares):
        cols = pl.ds(pl.multiple_of(j * 256, 256), 256)
        piece = resid_ref[:, cols].astype(f32) + jnp.dot(
            attn[...], big[pl.ds(0, ATTN), cols], preferred_element_type=f32
        )
        h[:, cols] = piece
        return squares + jnp.sum(piece * piece, axis=-1, keepdims=True)

    squares = lax.fori_loop(0, D // 256, project, jnp.zeros((T, 1), f32))
    inverse = lax.rsqrt(squares / D + 1e-05)
    ng = [[n_slot(hh, f) for f in range(2)] for hh in range(2)]
    for hh in range(2):
        rows = pl.ds(hh * T2, T2)
        nrm[n_rows(hh, me), :] = (
            h[rows, :] * inverse[hh * T2 : (hh + 1) * T2] * gain_ref[...]
        ).astype(bf16)
        if hh == 0:
            for f in range(2):
                spread(ng[0][f])

    def forward_weight(i):
        for k in range(1, X):
            s = rpeer(k)
            arrive(w_slot(i, s), w_recv.at[i, s])
            send(w_slot(i, s), w_slot(i, s), w_recv.at[i, s], "req", sibling)

    def weight_arrived(i):
        own_w[i].wait()
        for k in range(X):
            s = flip(x, k) * 2 + 1 - c
            arrive(w_slot(i, s), w_recv.at[i, s])

    forward_weight(0)
    for k in range(1, A):
        for f in range(2):
            forward(ng[0][f], k, True)
    for f in range(2):
        hop(ng[0][f])
    for f in range(2):
        spread(ng[1][f])
    forward_weight(1)
    weight_arrived(0)
    weight_arrived(1)

    H = A // 2
    pair = a // 2
    order = [*range(H - 1, 0, -1), 0]
    M = 4 * T2
    wide = 256 if Dq % 256 == 0 else Dq

    def g_rows(hh, g):
        return pl.ds(pl.multiple_of((hh * n + 4 * nearest(pair, H, order[g])) * T2, M), M)

    def gated(hh, g):
        rows = g_rows(hh, g)

        def step(j, carry):
            cols = pl.ds(pl.multiple_of(j * 256, 256), 256)
            gate = jnp.dot(nrm[rows, :], wgs[:, cols], preferred_element_type=f32)
            upper = jnp.dot(nrm[rows, :], wus[:, cols], preferred_element_type=f32)
            hid[g, :, cols] = (gate / (1.0 + jnp.exp(-gate)) * upper).astype(bf16)
            return carry

        lax.fori_loop(0, F // 256, step, 0)

    pieces = [(2 * x, 2)] + [(flip(x, k) * 2 + cc, 1) for k in range(1, X) for cc in range(2)]

    def p_cols(p):
        first, count = pieces[p]
        return pl.ds(pl.multiple_of(first * Dq, 128), count * Dq)

    def lowered(hh, g, p):
        rows = g_rows(hh, g)
        first, count = pieces[p]

        def step(j, carry):
            for i in range(Dq // wide):
                piece = jnp.dot(
                    hid[g], wds[first + j, :, i * wide : (i + 1) * wide], preferred_element_type=f32
                )
                cols = pl.ds(pl.multiple_of((first + j) * Dq + i * wide, 128), wide)
                big[rows, cols] = piece.astype(bf16)
            return carry

        lax.fori_loop(0, count, step, 0)

    def b_rows(hh, pos, plane):
        return n_rows(hh, pos * 2 + plane)

    def r_rows(hh, i):
        return pl.ds(pl.multiple_of((i * 2 + hh) * T2, T2), T2)

    def targets(g):
        there = nearest(pair, H, order[g])
        right = at_least(there, pair)
        return right, [2 * there + right, 2 * there + 1 - right]

    def y_at(hh, p, d):
        return yr.at[r_rows(hh, d), p_cols(p)], y_recv.at[hh * len(pieces) + p, d]

    def z_at(hh, p, i):
        return zr.at[r_rows(hh, i), p_cols(p)], z_recv.at[hh * len(pieces) + p, i]

    def cross(hh, p, d):
        dst, sem = y_at(hh, p, d)
        send(big.at[b_rows(hh, d, 1 - b), p_cols(p)], dst, sem, "mlp", partner)

    def add(rows, cols, *terms):
        total = big[rows, cols].astype(f32)
        for term in terms:
            total = total + term[...].astype(f32)
        big[rows, cols] = total.astype(bf16)

    def onward(hh, p, d, right, met, crossed):
        rows, cols = b_rows(hh, d, b), p_cols(p)
        z, zsem = z_at(hh, p, d)
        arrive(z, zsem, met)
        terms = []
        if crossed:
            y, ysem = y_at(hh, p, d)
            arrive(y, ysem)
            terms = [y]
            pl.when(jnp.logical_not(met))(lambda: add(rows, cols, y))
        pl.when(met)(lambda: add(rows, cols, *terms, z))
        to = a + 2 * right - 1
        into = d + (1 - right) * at_least(d, to) * (A - d)
        dst, sem = z_at(hh, p, into)
        send(big.at[rows, cols], dst, sem, "mlp", to * 2 + b)

    def far_out(hh, g, p):
        lowered(hh, g, p)
        for d in targets(g)[1]:
            cross(hh, p, d)

    def far_on(hh, g, p):
        right, ds = targets(g)
        met = ((right == 1) & has_l) | ((right == 0) & has_r)
        for d in ds:
            onward(hh, p, d, right, met, True)

    def near_out(hh, p):
        lowered(hh, H - 1, p)
        dst, sem = z_at(hh, p, A + 1)
        send(big.at[b_rows(hh, mate, 1 - b), p_cols(p)], dst, sem, "mlp", mate * 2 + b)

    def near_on(hh, p):
        right = at_least(mate, a)
        met = ((right == 1) & has_l) | ((right == 0) & has_r)
        onward(hh, p, mate, right, met, False)
        z, zsem = z_at(hh, p, A + 1)
        arrive(z, zsem)
        add(b_rows(hh, a, 1 - b), p_cols(p), z)
        cross(hh, p, a)

    def finish(hh, p):
        rows, cols = pl.ds(hh * T2, T2), p_cols(p)
        y, ysem = y_at(hh, p, a)
        zl, lsem = z_at(hh, p, a)
        zr_, rsem = z_at(hh, p, A)
        arrive(y, ysem)
        total = h[rows, cols] + (big[b_rows(hh, a, b), cols].astype(f32) + y[...].astype(f32))
        h[rows, cols] = total
        for z, sem, met in ((zl, lsem, has_l), (zr_, rsem, has_r)):
            arrive(z, sem, met)

            def plus(z=z):
                h[rows, cols] = h[rows, cols] + z[...].astype(f32)

            pl.when(met)(plus)
        out_ref[rows, cols] = h[rows, cols].astype(bf16)

    def down_arrived(k, cc):
        s = flip(x, k) * 2 + cc
        arrive(d_part(s, c), d_recv.at[s, c])
        send(d_part(s, c), d_part(s, c), d_recv.at[s, c], "req", sibling)
        arrive(d_part(s, 1 - c), d_recv.at[s, 1 - c])

    waiting = [(k, f) for k in range(1, A) for f in range(2)]

    def pass_on(count):
        for _ in range(count):
            if waiting:
                k, f = waiting.pop(0)
                forward(ng[1][f], k, True)

    for hh in range(2):
        if hh == 1:
            pass_on(len(waiting))
            for f in range(2):
                hop(ng[1][f])
        for f in range(2):
            for k in range(1, A):
                other(ng[hh][f], k)
        for g in range(H - 1):
            gated(hh, g)
            far_out(hh, g, 0)
            if hh == 0:
                pass_on(2)
        gated(hh, H - 1)
        near_out(hh, 0)
        for p in range(len(pieces)):
            if p > 0:
                if hh == 0:
                    down_arrived((p + 1) // 2, (p + 1) % 2)
                for g in range(H - 1):
                    far_out(hh, g, p)
                near_out(hh, p)
            for g in range(H - 1):
                far_on(hh, g, p)
            if hh == 0:
                pass_on(2)
            near_on(hh, p)
        for p in range(len(pieces)):
            finish(hh, p)
    for copy, when in started:
        if when is None:
            copy.wait_send()
        else:
            pl.when(when)(copy.wait_send)


def body(
    n, nr,
    resid, queries, fresh_keys, fresh_values, paged_key_cache, paged_value_cache,
    page_table, cache_lengths, out_weight, norm_gain, gate_weight, up_weight, down_weight,
):
    T, D = resid.shape
    own_pages, page_tokens = paged_key_cache.shape[:2]
    R = own_pages * page_tokens + T
    A, X = n // 2, nr // 2
    depth, F = gate_weight.shape
    Dq = down_weight.shape[1]
    pieces = nr - 1
    sends = 400
    bf16, f32 = jnp.bfloat16, jnp.float32
    dma = pltpu.SemaphoreType.DMA
    vmem = pl.BlockSpec(memory_space=pltpu.VMEM)
    smem = pl.BlockSpec(memory_space=pltpu.SMEM)
    hbm = pl.BlockSpec(memory_space=pl.ANY)
    return pl.pallas_call(
        functools.partial(kernel, n, nr),
        out_shape=jax.ShapeDtypeStruct((T, D), bf16),
        in_specs=[smem] * 2 + [vmem] * 3 + [hbm] * 8,
        out_specs=vmem,
        scratch_shapes=[
            pltpu.VMEM((n * R, KV_COLS), bf16),
            pltpu.VMEM((n * R, KV_COLS), bf16),
            pltpu.VMEM((n * T, D), bf16),
            pltpu.VMEM((nr * depth, F), bf16),
            pltpu.VMEM((nr * depth, F), bf16),
            pltpu.VMEM((nr, F, Dq), bf16),
            pltpu.VMEM((max(n * T, out_weight.shape[0]), D), bf16),
            pltpu.VMEM((A * T, D), bf16),
            pltpu.VMEM(((A + 2) * T, D), bf16),
            pltpu.VMEM((T, D), f32),
            pltpu.VMEM((T, ATTN), bf16),
            pltpu.VMEM((QUERY_HEADS // 2, 2 * T, 1), f32),
            pltpu.VMEM((QUERY_HEADS // 2, 2 * T, 1), f32),
            pltpu.VMEM((T, 2 * R), f32),
            pltpu.VMEM((A // 2, 2 * T, F), bf16),
            dma((4, max(own_pages + 1, 3))),
            dma((sends,)),
            dma((2, n)),
            dma((4, n)),
            dma((3, nr)),
            dma((nr, 2)),
            dma((2 * pieces, A)),
            dma((2 * pieces, A + 2)),
        ],
        compiler_params=pltpu.CompilerParams(
            collective_id=0, has_side_effects=True, vmem_limit_bytes=62 * 2**20
        ),
    )(
        page_table, cache_lengths, queries, resid, norm_gain.reshape(1, D), fresh_keys, fresh_values,
        paged_key_cache, paged_value_cache, out_weight, gate_weight, up_weight, down_weight,
    )


def solution(mesh):
    placed = (
        P(("req", "mlp"), None),
        P(("req", "mlp"), None),
        P(("req", "mlp"), None),
        P(("req", "mlp"), None),
        P(("req", "mlp"), None, None),
        P(("req", "mlp"), None, None),
        P("req", None),
        P("req"),
        P(),
        P(),
        P("req", "mlp"),
        P("req", "mlp"),
        P("mlp", "req"),
    )
    return jax.shard_map(
        functools.partial(body, mesh.shape["mlp"], mesh.shape["req"]),
        mesh=mesh, in_specs=placed, out_specs=P(("req", "mlp"), None), check_vma=False,
    )
```

```python
import functools
import math

import jax
import jax.numpy as jnp
from jax import lax
from jax.experimental import pallas as pl
from jax.experimental.pallas import tpu as pltpu
from jax.sharding import PartitionSpec as P

QUERY_HEADS = 12
KEY_VALUE_HEADS = 2
HEAD_SIZE = 128
GROUP = QUERY_HEADS // KEY_VALUE_HEADS
KV_COLS = KEY_VALUE_HEADS * HEAD_SIZE
ATTN = QUERY_HEADS * HEAD_SIZE
MESH = pl.DeviceIdType.MESH


def flip(a, k):
    bit = 1
    while bit <= k:
        if k & bit:
            a = a + bit - 2 * bit * (lax.rem(a // bit, 2))
        bit *= 2
    return a


def at_least(u, v):
    return (u - v + 1024) // 1024


def nearest(a, count, j):
    if j == 0:
        return a
    low = 1 - at_least(a, count // 2)
    room = low * a + (1 - low) * (count - 1 - a)
    both = at_least(2 * room, j)
    step = (j + 1) // 2
    return a + both * (-step if j % 2 else step) + (1 - both) * (2 * low - 1) * (j - room)


def kernel(
    n, nr,
    table, length, gain_ref, q_hbm, resid_hbm, fk, fv, pk, pv, ow, wg, wu, wd,
    out_hbm,
    q_ref, resid_ref, out_ref, kb, vb, nrm, wgs, wus, wds, big, yr, zr, h, attn, top, den, bias, hid,
    loc, ss, kv_recv, n_recv, w_recv, d_recv, y_recv, z_recv, out_sem,
):
    A, X = n // 2, nr // 2
    me, r = lax.axis_index("mlp"), lax.axis_index("req")
    a, b = me // 2, lax.rem(me, 2)
    x, c = r // 2, lax.rem(r, 2)
    partner, sibling = a * 2 + 1 - b, x * 2 + 1 - c
    mate = a + 1 - 2 * lax.rem(a, 2)
    has_l, has_r = a > 0, a < A - 1
    T, D = resid_ref.shape
    T2 = T // 2
    own_pages, page_tokens = pk.shape[:2]
    cached = own_pages * page_tokens
    R = cached + T
    depth, F = wg.shape
    Dq = wd.shape[1]
    bf16, f32 = jnp.bfloat16, jnp.float32

    def rpeer(k):
        return flip(x, k) * 2 + c

    def remote(src, dst, sem, recv_sem, axis, idx):
        return pltpu.make_async_remote_copy(
            src_ref=src, dst_ref=dst, send_sem=sem, recv_sem=recv_sem,
            device_id={axis: idx}, device_id_type=MESH,
        )

    started = []

    def send(src, dst, recv_sem, axis, idx, when=None):
        copy = remote(src, dst, ss.at[len(started)], recv_sem, axis, idx)
        started.append((copy, when))
        if when is None:
            copy.start()
        else:
            pl.when(when)(copy.start)

    def arrive(ref, recv_sem, when=None):
        copy = remote(ref, ref, recv_sem, recv_sem, "mlp", partner)
        if when is None:
            copy.wait_recv()
        else:
            pl.when(when)(copy.wait_recv)

    base = pl.multiple_of(me * R, 128)
    mine = []
    for i, (buf, pages, fresh) in enumerate(((kb, pk, fk), (vb, pv, fv))):
        for j in range(own_pages):
            mine.append(pltpu.make_async_copy(
                pages.at[j], buf.at[pl.ds(base + j * page_tokens, page_tokens), :], loc.at[i, j]))
        mine.append(pltpu.make_async_copy(fresh, buf.at[pl.ds(base + cached, T), :], loc.at[i, own_pages]))
    for copy in mine:
        copy.start()

    def w_slot(i, s):
        if i == 2:
            return wds.at[s]
        buf = wgs if i == 0 else wus
        return buf.at[pl.ds(pl.multiple_of(s * depth, 128), depth), :]

    quarter = depth // 4

    def w_part(i, s, j):
        buf = wgs if i == 0 else wus
        return buf.at[pl.ds(pl.multiple_of(s * depth + j * quarter, 16), quarter), :]

    weights = (wg, wu, wd)
    own_w = [pltpu.make_async_copy(weights[i], w_slot(i, r), loc.at[2, i]) for i in range(3)]
    own_q = pltpu.make_async_copy(q_hbm, q_ref, loc.at[3, 1])
    own_resid = pltpu.make_async_copy(resid_hbm, resid_ref, loc.at[3, 2])
    own_ow = pltpu.make_async_copy(ow, big.at[pl.ds(0, ATTN), :], loc.at[3, 0])

    own_q.start()
    own_resid.start()
    barrier = pltpu.get_barrier_semaphore()

    def greet(axis, idx):
        pl.semaphore_signal(barrier, inc=1, device_id={axis: idx}, device_id_type=MESH)

    greet("mlp", partner)
    greet("req", sibling)
    for k in range(1, X):
        greet("req", rpeer(k))
    pl.when(has_l)(lambda: greet("mlp", me - 2))
    pl.when(has_r)(lambda: greet("mlp", me + 2))
    pl.semaphore_wait(barrier, X + 1 + has_l.astype(jnp.int32) + has_r.astype(jnp.int32))

    def kv_slot(part):
        buf = (kb, vb)[part]
        return lambda s: buf.at[pl.ds(pl.multiple_of(s * R, 128), R), :], lambda s: kv_recv.at[part, s]

    half = D // 2

    def n_rows(hh, s):
        return pl.ds(pl.multiple_of((hh * n + s) * T2, T2), T2)

    def n_slot(hh, f):
        return (
            lambda s: nrm.at[n_rows(hh, s), pl.ds(f * half, half)],
            lambda s: n_recv.at[hh * 2 + f, s],
        )

    def along(kind, when=True):
        slot, sem = kind
        send(slot(me), slot(me), sem(me), "mlp", me + 2, has_r & when)
        send(slot(me), slot(me), sem(me), "mlp", me - 2, has_l & when)

    def across(kind):
        slot, sem = kind
        send(slot(me), slot(me), sem(me), "mlp", partner)

    def spread(kind):
        along(kind)
        across(kind)

    end = (a == 0) | (a == A - 1)
    mid = jnp.logical_not(end)

    def hopped(pos):
        return (pos <= a + 1) & (pos >= a - 1) & (pos != a) & (pos > 0) & (pos < A - 1)

    def forward(kind, k, hops, when=True):
        slot, sem = kind
        pos = nearest(a, A, k)
        s = pos * 2 + b
        arrive(slot(s), sem(s), None if when is True else when)
        right = at_least(a, pos)
        to = a + 2 * right - 1
        send(slot(s), slot(s), sem(s), "mlp", to * 2 + b, (to >= 0) & (to < A) & when)
        crosses = jnp.logical_not(hopped(pos)) & when if hops else (None if when is True else when)
        send(slot(s), slot(s), sem(s), "mlp", partner, crosses)

    def hop(kind):
        slot, sem = kind
        arrive(slot(partner), sem(partner))
        for to, there in ((a + 1, has_r), (a - 1, has_l)):
            send(slot(partner), slot(partner), sem(partner), "mlp", to * 2 + b, there & mid)

    def other(kind, pos):
        slot, sem = kind
        s = pos * 2 + 1 - b
        arrive(slot(s), sem(s))

    kv = [kv_slot(0), kv_slot(1)]
    for part in range(2):
        for copy in mine[part * (own_pages + 1) : (part + 1) * (own_pages + 1)]:
            copy.wait()
        spread(kv[part])
    for i in range(2):
        for k in range(1, X):
            for j in range(4):
                part = weights[i].at[pl.ds(j * quarter, quarter), :]
                send(part, w_part(i, r, j), w_recv.at[i, r, j], "req", rpeer(k))
    own_w[2].start()
    send(wd, w_slot(2, r), w_recv.at[2, r, 0], "req", sibling)
    own_ow.start()
    for i in range(2):
        own_w[i].start()
        send(weights[i], w_slot(i, r), w_recv.at[i, r, 0], "req", sibling)

    factor = HEAD_SIZE ** (-0.5) * math.log2(math.e)
    ahead = lax.broadcasted_iota(jnp.int32, (T, T), 1) - lax.broadcasted_iota(jnp.int32, (T, T), 0)
    lane = lax.broadcasted_iota(jnp.int32, (T, page_tokens), 1)

    def mask(pos):
        for j in range(2):
            s = pos * 2 + j
            for p in range(own_pages):
                page = jnp.int32(0)
                for i in range(table.shape[1]):
                    page = page + jnp.where(table[0, i] == s * own_pages + p, i, 0)
                live = lane < length[0] - page * page_tokens
                bias[:, j * R + p * page_tokens : j * R + (p + 1) * page_tokens] = jnp.where(live, 0.0, -1e30)
            bias[:, j * R + cached : (j + 1) * R] = jnp.where(ahead <= (me - s) * T, 0.0, -1e30)

    def attend(pos, last=False):
        rows = pl.ds(pl.multiple_of(pos * 2 * R, 128), 2 * R)

        def step(i, carry):
            head = 2 * i
            g = head // GROUP
            c0 = pl.ds(pl.multiple_of(head * HEAD_SIZE, 128), HEAD_SIZE)
            c1 = pl.ds(pl.multiple_of(head * HEAD_SIZE + HEAD_SIZE, 128), HEAD_SIZE)
            gc = pl.ds(pl.multiple_of(g * HEAD_SIZE, 128), HEAD_SIZE)
            qq = jnp.concatenate([q_ref[:, c0], q_ref[:, c1]], axis=0)
            s = lax.dot_general(
                qq, kb[rows, gc], (((1,), (1,)), ((), ())), preferred_element_type=f32
            )
            s = ((s * factor).reshape(2, T, 2 * R) + bias[...][None]).reshape(2 * T, 2 * R)
            before = top[i]
            most = jnp.maximum(jnp.max(s, axis=-1, keepdims=True), before)
            scale = jnp.exp2(before - most)
            e = jnp.exp2(s - most)
            total = jnp.sum(e, axis=-1, keepdims=True) + den[i] * scale
            o = jnp.dot(e.astype(bf16), vb[rows, gc], preferred_element_type=f32)
            o = o + jnp.concatenate([h[:, c0], h[:, c1]], axis=0) * scale
            if last:
                o = o / total
                attn[:, c0] = o[:T].astype(bf16)
                attn[:, c1] = o[T:].astype(bf16)
            else:
                top[i] = most
                den[i] = total
                h[:, c0] = o[:T]
                h[:, c1] = o[T:]
            return carry

        lax.fori_loop(0, QUERY_HEADS // 2, step, 0, unroll=2)

    def both(f, *args):
        for part in range(2):
            f(kv[part], *args)

    def stage(pos, last=False):
        mask(pos)
        both(other, pos)
        attend(pos, last)

    ended = 1 - at_least(a, 1) + at_least(a, A - 1)

    def turn(k):
        return ended * nearest(a, A, k - 1) + (1 - ended) * nearest(a, A, max(k - 2, 0))

    top[...] = jnp.full_like(top, -2e30)
    den[...] = jnp.zeros_like(den)
    h[...] = jnp.zeros_like(h)
    fh = F // 2

    def d_part(s, part):
        return wds.at[s, pl.ds(pl.multiple_of(part * fh, 16), fh), :]

    own_q.wait()
    own_resid.wait()
    for k in range(1, A):
        both(forward, k, False)
        if k == 1:
            pl.when(end)(lambda: stage(nearest(a, A, 0)))
            own_w[2].wait()
            arrive(w_slot(2, sibling), w_recv.at[2, sibling, 0])
            for cc in range(2):
                for kk in range(1, X):
                    s = x * 2 + cc
                    send(d_part(s, c), d_part(s, c), d_recv.at[s, c], "req", rpeer(kk))
        else:
            stage(turn(k))
    pl.when(mid)(lambda: stage(nearest(a, A, A - 2)))
    stage(nearest(a, A, A - 1), True)

    own_ow.wait()

    def project(j, squares):
        cols = pl.ds(pl.multiple_of(j * 256, 256), 256)
        piece = resid_ref[:, cols].astype(f32) + jnp.dot(
            attn[...], big[pl.ds(0, ATTN), cols], preferred_element_type=f32
        )
        h[:, cols] = piece
        return squares + jnp.sum(piece * piece, axis=-1, keepdims=True)

    squares = lax.fori_loop(0, D // 256, project, jnp.zeros((T, 1), f32), unroll=4)
    inverse = lax.rsqrt(squares / D + 1e-05)
    ng = [[n_slot(hh, f) for f in range(2)] for hh in range(2)]
    for hh in range(2):
        rows = pl.ds(hh * T2, T2)
        nrm[n_rows(hh, me), :] = (
            h[rows, :] * inverse[hh * T2 : (hh + 1) * T2] * gain_ref[...]
        ).astype(bf16)
        for f in range(2):
            if hh == 0:
                spread(ng[0][f])
            else:
                across(ng[1][f])
                along(ng[1][f], end)

    def forward_weight(i, when=None):
        for k in range(1, X):
            s = rpeer(k)
            for j in range(4):
                arrive(w_part(i, s, j), w_recv.at[i, s, j], when)
                send(w_part(i, s, j), w_part(i, s, j), w_recv.at[i, s, j], "req", sibling, when)

    def weight_arrived(i):
        own_w[i].wait()
        arrive(w_slot(i, sibling), w_recv.at[i, sibling, 0])
        for k in range(1, X):
            s = flip(x, k) * 2 + 1 - c
            for j in range(4):
                arrive(w_part(i, s, j), w_recv.at[i, s, j])

    forward_weight(0)
    for k in range(1, A):
        if k == A - 1:
            forward_weight(1, end)
        for f in range(2):
            forward(ng[0][f], k, True)
    for f in range(2):
        hop(ng[0][f])
    for f in range(2):
        along(ng[1][f], mid)
    forward_weight(1, mid)
    weight_arrived(0)
    weight_arrived(1)

    H = A // 2
    pair = a // 2
    order = [*range(H - 1, 0, -1), 0]
    M = 4 * T2
    wide = 256 if Dq % 256 == 0 else Dq

    def g_rows(hh, g):
        return pl.ds(pl.multiple_of((hh * n + 4 * nearest(pair, H, order[g])) * T2, M), M)

    def gated(hh, g):
        rows = g_rows(hh, g)

        def step(j, carry):
            cols = pl.ds(pl.multiple_of(j * 256, 256), 256)
            gate = jnp.dot(nrm[rows, :], wgs[:, cols], preferred_element_type=f32)
            upper = jnp.dot(nrm[rows, :], wus[:, cols], preferred_element_type=f32)
            hid[g, :, cols] = (gate / (1.0 + jnp.exp(-gate)) * upper).astype(bf16)
            return carry

        lax.fori_loop(0, F // 256, step, 0, unroll=2)

    pieces = [flip(x, k) * 2 + cc for k in range(X) for cc in range(2)]

    def p_cols(p):
        return pl.ds(pl.multiple_of(pieces[p] * Dq, 128), Dq)

    def lowered(hh, g, p):
        rows = g_rows(hh, g)
        for i in range(Dq // wide):
            piece = jnp.dot(
                hid[g], wds[pieces[p], :, i * wide : (i + 1) * wide], preferred_element_type=f32
            )
            cols = pl.ds(pl.multiple_of(pieces[p] * Dq + i * wide, 128), wide)
            big[rows, cols] = piece.astype(bf16)

    def b_rows(hh, pos, plane):
        return n_rows(hh, pos * 2 + plane)

    def r_rows(hh, i):
        return pl.ds(pl.multiple_of((i * 2 + hh) * T2, T2), T2)

    def targets(g):
        there = nearest(pair, H, order[g])
        right = at_least(there, pair)
        return right, [2 * there + right, 2 * there + 1 - right]

    def y_at(hh, p, d):
        return yr.at[r_rows(hh, d), p_cols(p)], y_recv.at[hh * len(pieces) + p, d]

    def z_at(hh, p, i):
        return zr.at[r_rows(hh, i), p_cols(p)], z_recv.at[hh * len(pieces) + p, i]

    def cross(hh, p, d):
        dst, sem = y_at(hh, p, d)
        send(big.at[b_rows(hh, d, 1 - b), p_cols(p)], dst, sem, "mlp", partner)

    def add(rows, cols, *terms):
        total = big[rows, cols].astype(f32)
        for term in terms:
            total = total + term[...].astype(f32)
        big[rows, cols] = total.astype(bf16)

    def fed(d):
        return ((d > a) & has_l) | ((d < a) & has_r)

    def out(hh, p, d):
        src = big.at[b_rows(hh, d, 1 - b), p_cols(p)]
        right = at_least(d, a)
        dst, sem = z_at(hh, p, A + 2 - right)
        send(src, dst, sem, "mlp", (a + 2 * right - 1) * 2 + b, hopped(d))
        dst, sem = y_at(hh, p, d)
        send(src, dst, sem, "mlp", partner, jnp.logical_not(hopped(d)))

    def onward(hh, p, d, when=True):
        rows, cols = b_rows(hh, d, b), p_cols(p)
        right = at_least(d, a)
        z, zsem = z_at(hh, p, d)
        y, ysem = y_at(hh, p, d)
        zin, yin = fed(d) & when, jnp.logical_not(hopped(d)) & when
        arrive(z, zsem, zin)
        arrive(y, ysem, yin)
        pl.when(yin & zin)(lambda: add(rows, cols, y, z))
        pl.when(yin & jnp.logical_not(zin))(lambda: add(rows, cols, y))
        pl.when(zin & jnp.logical_not(yin))(lambda: add(rows, cols, z))
        to = a + 2 * right - 1
        into = d + (1 - right) * at_least(d, to) * (A - d)
        dst, sem = z_at(hh, p, into)
        send(big.at[rows, cols], dst, sem, "mlp", to * 2 + b, None if when is True else when)

    def far_out(hh, g, p):
        lowered(hh, g, p)
        for d in targets(g)[1]:
            out(hh, p, d)

    def far_on(hh, g, p):
        for d in targets(g)[1]:
            onward(hh, p, d)

    free = jnp.logical_not(fed(mate)) & hopped(mate)

    def near_out(hh, p):
        lowered(hh, H - 1, p)
        out(hh, p, mate)
        onward(hh, p, mate, free)

    def mate_on(hh, p):
        onward(hh, p, mate, jnp.logical_not(free))

    def own_on(hh, p):
        for d, i in ((a - 1, A + 1), (a + 1, A + 2)):
            z, zsem = z_at(hh, p, i)
            met = (d >= 0) & (d < A) & mid
            arrive(z, zsem, met)
            pl.when(met)(lambda z=z: add(b_rows(hh, a, 1 - b), p_cols(p), z))
        cross(hh, p, a)

    outs = []

    def finish(hh, p):
        rows, cols = pl.ds(hh * T2, T2), p_cols(p)
        y, ysem = y_at(hh, p, a)
        zl, lsem = z_at(hh, p, a)
        zr_, rsem = z_at(hh, p, A)
        arrive(y, ysem)
        total = h[rows, cols] + (big[b_rows(hh, a, b), cols].astype(f32) + y[...].astype(f32))
        h[rows, cols] = total
        for z, sem, met in ((zl, lsem, has_l), (zr_, rsem, has_r)):
            arrive(z, sem, met)

            def plus(z=z):
                h[rows, cols] = h[rows, cols] + z[...].astype(f32)

            pl.when(met)(plus)
        out_ref[rows, cols] = h[rows, cols].astype(bf16)
        copy = pltpu.make_async_copy(out_ref.at[rows, cols], out_hbm.at[rows, cols], out_sem.at[hh, p])
        copy.start()
        outs.append(copy)

    def down_forward(p):
        s = pieces[p]
        arrive(d_part(s, c), d_recv.at[s, c])
        send(d_part(s, c), d_part(s, c), d_recv.at[s, c], "req", sibling)

    def down_arrived(p):
        s = pieces[p]
        arrive(d_part(s, 1 - c), d_recv.at[s, 1 - c])

    def pass_on(k, when=True):
        for f in range(2):
            forward(ng[1][f], k, True, when)

    count = len(pieces)
    far = range(H - 1)

    def others(hh, g):
        there = nearest(pair, H, order[g])
        for f in range(2):
            if g < H - 1:
                other(ng[hh][f], 2 * there)
                other(ng[hh][f], 2 * there + 1)
            else:
                other(ng[hh][f], mate)

    others(0, H - 1)
    gated(0, H - 1)
    for p in range(2):
        near_out(0, p)
    for k in range(1, A - 1):
        pass_on(k, mid)
    for g in far:
        others(0, g)
        gated(0, g)
        for p in range(2):
            far_out(0, g, p)
    pass_on(1, end)
    down_forward(2)
    for p in range(2):
        own_on(0, p)
    pass_on(A - 1, mid)
    for f in range(2):
        hop(ng[1][f])
    for p in range(2):
        for g in far:
            far_on(0, g, p)
        mate_on(0, p)
    for k in range(2, A - 1):
        pass_on(k, end)
    for p in range(3, count):
        down_forward(p)
    for p in range(2, count):
        down_arrived(p)
        near_out(0, p)
        for g in far:
            far_out(0, g, p)
    pass_on(A - 1, end)
    for p in range(2, count):
        own_on(0, p)
        for g in far:
            far_on(0, g, p)
        if p == 2:
            others(1, H - 1)
            gated(1, H - 1)
            for q in range(2):
                near_out(1, q)
    for p in range(2, count):
        mate_on(0, p)
    for g in far:
        others(1, g)
        gated(1, g)
        for p in range(2):
            far_out(1, g, p)
    for p in range(2, count):
        for g in far:
            far_out(1, g, p)
        near_out(1, p)
    for p in range(count):
        own_on(1, p)
        for g in far:
            far_on(1, g, p)
        mate_on(1, p)
    for hh in range(2):
        for p in range(count):
            finish(hh, p)
    for copy in outs:
        copy.wait()
    for copy, when in started:
        if when is None:
            copy.wait_send()
        else:
            pl.when(when)(copy.wait_send)


def body(
    n, nr,
    resid, queries, fresh_keys, fresh_values, paged_key_cache, paged_value_cache,
    page_table, cache_lengths, out_weight, norm_gain, gate_weight, up_weight, down_weight,
):
    T, D = resid.shape
    own_pages, page_tokens = paged_key_cache.shape[:2]
    R = own_pages * page_tokens + T
    A, X = n // 2, nr // 2
    depth, F = gate_weight.shape
    Dq = down_weight.shape[1]
    pieces = nr
    sends = 400
    bf16, f32 = jnp.bfloat16, jnp.float32
    dma = pltpu.SemaphoreType.DMA
    vmem = pl.BlockSpec(memory_space=pltpu.VMEM)
    smem = pl.BlockSpec(memory_space=pltpu.SMEM)
    hbm = pl.BlockSpec(memory_space=pl.ANY)
    return pl.pallas_call(
        functools.partial(kernel, n, nr),
        out_shape=jax.ShapeDtypeStruct((T, D), bf16),
        in_specs=[smem] * 2 + [vmem] + [hbm] * 10,
        out_specs=hbm,
        scratch_shapes=[
            pltpu.VMEM((T, ATTN), bf16),
            pltpu.VMEM((T, D), bf16),
            pltpu.VMEM((T, D), bf16),
            pltpu.VMEM((n * R, KV_COLS), bf16),
            pltpu.VMEM((n * R, KV_COLS), bf16),
            pltpu.VMEM((n * T, D), bf16),
            pltpu.VMEM((nr * depth, F), bf16),
            pltpu.VMEM((nr * depth, F), bf16),
            pltpu.VMEM((nr, F, Dq), bf16),
            pltpu.VMEM((max(n * T, out_weight.shape[0]), D), bf16),
            pltpu.VMEM((A * T, D), bf16),
            pltpu.VMEM(((A + 3) * T, D), bf16),
            pltpu.VMEM((T, D), f32),
            pltpu.VMEM((T, ATTN), bf16),
            pltpu.VMEM((QUERY_HEADS // 2, 2 * T, 1), f32),
            pltpu.VMEM((QUERY_HEADS // 2, 2 * T, 1), f32),
            pltpu.VMEM((T, 2 * R), f32),
            pltpu.VMEM((A // 2, 2 * T, F), bf16),
            dma((4, max(own_pages + 1, 3))),
            dma((sends,)),
            dma((2, n)),
            dma((4, n)),
            dma((3, nr, 4)),
            dma((nr, 2)),
            dma((2 * pieces, A)),
            dma((2 * pieces, A + 3)),
            dma((2, pieces)),
        ],
        compiler_params=pltpu.CompilerParams(
            collective_id=0, has_side_effects=True, vmem_limit_bytes=62 * 2**20
        ),
    )(
        page_table, cache_lengths, norm_gain.reshape(1, D), queries, resid, fresh_keys, fresh_values,
        paged_key_cache, paged_value_cache, out_weight, gate_weight, up_weight, down_weight,
    )


def solution(mesh):
    placed = (
        P(("req", "mlp"), None),
        P(("req", "mlp"), None),
        P(("req", "mlp"), None),
        P(("req", "mlp"), None),
        P(("req", "mlp"), None, None),
        P(("req", "mlp"), None, None),
        P("req", None),
        P("req"),
        P(),
        P(),
        P("req", "mlp"),
        P("req", "mlp"),
        P("mlp", "req"),
    )
    return jax.shard_map(
        functools.partial(body, mesh.shape["mlp"], mesh.shape["req"]),
        mesh=mesh, in_specs=placed, out_specs=P(("req", "mlp"), None), check_vma=False,
    )
```

```python
import functools
import math

import jax
import jax.numpy as jnp
from jax import lax
from jax.experimental import pallas as pl
from jax.experimental.pallas import tpu as pltpu
from jax.sharding import PartitionSpec as P

QUERY_HEADS = 12
KEY_VALUE_HEADS = 2
HEAD_SIZE = 128
GROUP = QUERY_HEADS // KEY_VALUE_HEADS
KV_COLS = KEY_VALUE_HEADS * HEAD_SIZE
ATTN = QUERY_HEADS * HEAD_SIZE
MESH = pl.DeviceIdType.MESH


def flip(a, k):
    bit = 1
    while bit <= k:
        if k & bit:
            a = a + bit - 2 * bit * (lax.rem(a // bit, 2))
        bit *= 2
    return a


def at_least(u, v):
    return (u - v + 1024) // 1024


def nearest(a, count, j):
    if j == 0:
        return a
    low = 1 - at_least(a, count // 2)
    room = low * a + (1 - low) * (count - 1 - a)
    both = at_least(2 * room, j)
    step = (j + 1) // 2
    return a + both * (-step if j % 2 else step) + (1 - both) * (2 * low - 1) * (j - room)


def kernel(
    n, nr,
    table, length, gain_ref, q_hbm, resid_hbm, fk, fv, pk, pv, ow, wg, wu, wd,
    out_hbm,
    q_ref, resid_ref, out_ref, kb, vb, nrm, wgs, wus, wds, big, yr, zr, h, attn, top, den, bias, hid,
    loc, ss, sx, kv_recv, n_recv, w_recv, d_recv, y_recv, z_recv, out_sem,
):
    A, X = n // 2, nr // 2
    me, r = lax.axis_index("mlp"), lax.axis_index("req")
    a, b = me // 2, lax.rem(me, 2)
    x, c = r // 2, lax.rem(r, 2)
    partner, sibling = a * 2 + 1 - b, x * 2 + 1 - c
    mate = a + 1 - 2 * lax.rem(a, 2)
    has_l, has_r = a > 0, a < A - 1
    T, D = resid_ref.shape
    T2 = T // 2
    own_pages, page_tokens = pk.shape[:2]
    cached = own_pages * page_tokens
    R = cached + T
    depth, F = wg.shape
    Dq = wd.shape[1]
    bf16, f32 = jnp.bfloat16, jnp.float32

    def rpeer(k):
        return flip(x, k) * 2 + c

    def remote(src, dst, sem, recv_sem, axis, idx):
        return pltpu.make_async_remote_copy(
            src_ref=src, dst_ref=dst, send_sem=sem, recv_sem=recv_sem,
            device_id={axis: idx}, device_id_type=MESH,
        )

    ring = ss.shape[0]
    started, slow = [], []

    def sent(copy, when):
        if when is None:
            copy.wait_send()
        else:
            pl.when(when)(copy.wait_send)

    def send(src, dst, recv_sem, axis, idx, when=None, sem=None):
        if sem is None:
            if len(started) >= ring:
                sent(*started[-ring])
            sem = ss.at[len(started) % ring]
            kept = started
        else:
            kept = slow
        copy = remote(src, dst, sem, recv_sem, axis, idx)
        kept.append((copy, when))
        if when is None:
            copy.start()
        else:
            pl.when(when)(copy.start)

    def arrive(ref, recv_sem, when=None):
        copy = remote(ref, ref, recv_sem, recv_sem, "mlp", partner)
        if when is None:
            copy.wait_recv()
        else:
            pl.when(when)(copy.wait_recv)

    base = pl.multiple_of(me * R, 128)
    mine = []
    for i, (buf, pages, fresh) in enumerate(((kb, pk, fk), (vb, pv, fv))):
        for j in range(own_pages):
            mine.append(pltpu.make_async_copy(
                pages.at[j], buf.at[pl.ds(base + j * page_tokens, page_tokens), :], loc.at[i, j]))
        mine.append(pltpu.make_async_copy(fresh, buf.at[pl.ds(base + cached, T), :], loc.at[i, own_pages]))
    for copy in mine:
        copy.start()

    def w_slot(i, s):
        if i == 2:
            return wds.at[s]
        buf = wgs if i == 0 else wus
        return buf.at[pl.ds(pl.multiple_of(s * depth, 128), depth), :]

    quarter = depth // 4

    def w_part(i, s, j):
        buf = wgs if i == 0 else wus
        return buf.at[pl.ds(pl.multiple_of(s * depth + j * quarter, 16), quarter), :]

    weights = (wg, wu, wd)
    own_w = [pltpu.make_async_copy(weights[i], w_slot(i, r), loc.at[2, i]) for i in range(3)]
    own_q = pltpu.make_async_copy(q_hbm, q_ref, loc.at[3, 1])
    own_resid = pltpu.make_async_copy(resid_hbm, resid_ref, loc.at[3, 2])
    own_ow = pltpu.make_async_copy(ow, big.at[pl.ds(0, ATTN), :], loc.at[3, 0])

    own_q.start()
    own_resid.start()
    barrier = pltpu.get_barrier_semaphore()

    def greet(axis, idx):
        pl.semaphore_signal(barrier, inc=1, device_id={axis: idx}, device_id_type=MESH)

    greet("mlp", partner)
    greet("req", sibling)
    for k in range(1, X):
        greet("req", rpeer(k))
    pl.when(has_l)(lambda: greet("mlp", me - 2))
    pl.when(has_r)(lambda: greet("mlp", me + 2))
    pl.semaphore_wait(barrier, X + 1 + has_l.astype(jnp.int32) + has_r.astype(jnp.int32))

    def kv_slot(part):
        buf = (kb, vb)[part]
        return lambda s: buf.at[pl.ds(pl.multiple_of(s * R, 128), R), :], lambda s: kv_recv.at[part, s]

    half = D // 2

    def n_rows(hh, s):
        return pl.ds(pl.multiple_of((hh * n + s) * T2, T2), T2)

    def n_slot(hh, f):
        return (
            lambda s: nrm.at[n_rows(hh, s), pl.ds(f * half, half)],
            lambda s: n_recv.at[hh * 2 + f, s],
        )

    def along(kind, when=True):
        slot, sem = kind
        send(slot(me), slot(me), sem(me), "mlp", me + 2, has_r & when)
        send(slot(me), slot(me), sem(me), "mlp", me - 2, has_l & when)

    def across(kind):
        slot, sem = kind
        send(slot(me), slot(me), sem(me), "mlp", partner)

    def spread(kind):
        along(kind)
        across(kind)

    end = (a == 0) | (a == A - 1)
    mid = jnp.logical_not(end)

    def hopped(pos):
        return (pos <= a + 1) & (pos >= a - 1) & (pos != a) & (pos > 0) & (pos < A - 1)

    def forward(kind, k, hops, when=True):
        slot, sem = kind
        pos = nearest(a, A, k)
        s = pos * 2 + b
        arrive(slot(s), sem(s), None if when is True else when)
        right = at_least(a, pos)
        to = a + 2 * right - 1
        send(slot(s), slot(s), sem(s), "mlp", to * 2 + b, (to >= 0) & (to < A) & when)
        crosses = jnp.logical_not(hopped(pos)) & when if hops else (None if when is True else when)
        send(slot(s), slot(s), sem(s), "mlp", partner, crosses)

    def hop(kind):
        slot, sem = kind
        arrive(slot(partner), sem(partner))
        for to, there in ((a + 1, has_r), (a - 1, has_l)):
            send(slot(partner), slot(partner), sem(partner), "mlp", to * 2 + b, there & mid)

    def other(kind, pos):
        slot, sem = kind
        s = pos * 2 + 1 - b
        arrive(slot(s), sem(s))

    kv = [kv_slot(0), kv_slot(1)]
    for part in range(2):
        for copy in mine[part * (own_pages + 1) : (part + 1) * (own_pages + 1)]:
            copy.wait()
        spread(kv[part])
    for i in range(2):
        for k in range(1, X):
            for j in range(4):
                part = weights[i].at[pl.ds(j * quarter, quarter), :]
                send(part, w_part(i, r, j), w_recv.at[i, r, j], "req", rpeer(k), sem=sx.at[k, i * 4 + j])
    own_w[2].start()
    send(wd, w_slot(2, r), w_recv.at[2, r, 0], "req", sibling)
    own_ow.start()
    for i in range(2):
        own_w[i].start()
        send(weights[i], w_slot(i, r), w_recv.at[i, r, 0], "req", sibling)

    factor = HEAD_SIZE ** (-0.5) * math.log2(math.e)
    ahead = lax.broadcasted_iota(jnp.int32, (T, T), 1) - lax.broadcasted_iota(jnp.int32, (T, T), 0)
    lane = lax.broadcasted_iota(jnp.int32, (T, page_tokens), 1)

    def mask(pos):
        for j in range(2):
            s = pos * 2 + j
            for p in range(own_pages):
                page = jnp.int32(0)
                for i in range(table.shape[1]):
                    page = page + jnp.where(table[0, i] == s * own_pages + p, i, 0)
                live = lane < length[0] - page * page_tokens
                bias[:, j * R + p * page_tokens : j * R + (p + 1) * page_tokens] = jnp.where(live, 0.0, -1e30)
            bias[:, j * R + cached : (j + 1) * R] = jnp.where(ahead <= (me - s) * T, 0.0, -1e30)

    def attend(pos, last=False):
        rows = pl.ds(pl.multiple_of(pos * 2 * R, 128), 2 * R)

        def step(i, carry):
            head = 2 * i
            g = head // GROUP
            c0 = pl.ds(pl.multiple_of(head * HEAD_SIZE, 128), HEAD_SIZE)
            c1 = pl.ds(pl.multiple_of(head * HEAD_SIZE + HEAD_SIZE, 128), HEAD_SIZE)
            gc = pl.ds(pl.multiple_of(g * HEAD_SIZE, 128), HEAD_SIZE)
            qq = jnp.concatenate([q_ref[:, c0], q_ref[:, c1]], axis=0)
            s = lax.dot_general(
                qq, kb[rows, gc], (((1,), (1,)), ((), ())), preferred_element_type=f32
            )
            s = ((s * factor).reshape(2, T, 2 * R) + bias[...][None]).reshape(2 * T, 2 * R)
            before = top[i]
            most = jnp.maximum(jnp.max(s, axis=-1, keepdims=True), before)
            scale = jnp.exp2(before - most)
            e = jnp.exp2(s - most)
            total = jnp.sum(e, axis=-1, keepdims=True) + den[i] * scale
            o = jnp.dot(e.astype(bf16), vb[rows, gc], preferred_element_type=f32)
            o = o + jnp.concatenate([h[:, c0], h[:, c1]], axis=0) * scale
            if last:
                o = o / total
                attn[:, c0] = o[:T].astype(bf16)
                attn[:, c1] = o[T:].astype(bf16)
            else:
                top[i] = most
                den[i] = total
                h[:, c0] = o[:T]
                h[:, c1] = o[T:]
            return carry

        lax.fori_loop(0, QUERY_HEADS // 2, step, 0, unroll=2)

    def both(f, *args):
        for part in range(2):
            f(kv[part], *args)

    def stage(pos, last=False):
        mask(pos)
        both(other, pos)
        attend(pos, last)

    ended = 1 - at_least(a, 1) + at_least(a, A - 1)

    def turn(k):
        return ended * nearest(a, A, k - 1) + (1 - ended) * nearest(a, A, max(k - 2, 0))

    top[...] = jnp.full_like(top, -2e30)
    den[...] = jnp.zeros_like(den)
    h[...] = jnp.zeros_like(h)
    fh = F // 2

    def d_part(s, part):
        return wds.at[s, pl.ds(pl.multiple_of(part * fh, 16), fh), :]

    own_q.wait()
    own_resid.wait()
    for k in range(1, A):
        both(forward, k, False)
        if k == 1:
            pl.when(end)(lambda: stage(nearest(a, A, 0)))
            own_w[2].wait()
            arrive(w_slot(2, sibling), w_recv.at[2, sibling, 0])
            for cc in range(2):
                for kk in range(1, X):
                    s = x * 2 + cc
                    send(d_part(s, c), d_part(s, c), d_recv.at[s, c], "req", rpeer(kk), sem=sx.at[kk, 8 + cc])
        else:
            stage(turn(k))
    pl.when(mid)(lambda: stage(nearest(a, A, A - 2)))
    stage(nearest(a, A, A - 1), True)

    own_ow.wait()

    def project(j, squares):
        cols = pl.ds(pl.multiple_of(j * 256, 256), 256)
        piece = resid_ref[:, cols].astype(f32) + jnp.dot(
            attn[...], big[pl.ds(0, ATTN), cols], preferred_element_type=f32
        )
        h[:, cols] = piece
        return squares + jnp.sum(piece * piece, axis=-1, keepdims=True)

    squares = lax.fori_loop(0, D // 256, project, jnp.zeros((T, 1), f32), unroll=4)
    inverse = lax.rsqrt(squares / D + 1e-05)
    ng = [[n_slot(hh, f) for f in range(2)] for hh in range(2)]
    for hh in range(2):
        rows = pl.ds(hh * T2, T2)
        nrm[n_rows(hh, me), :] = (
            h[rows, :] * inverse[hh * T2 : (hh + 1) * T2] * gain_ref[...]
        ).astype(bf16)
        for f in range(2):
            if hh == 0:
                spread(ng[0][f])
            else:
                across(ng[1][f])
                along(ng[1][f], end)

    def forward_weight(i, when=None):
        for k in range(1, X):
            s = rpeer(k)
            for j in range(4):
                arrive(w_part(i, s, j), w_recv.at[i, s, j], when)
                send(w_part(i, s, j), w_part(i, s, j), w_recv.at[i, s, j], "req", sibling, when)

    def weight_arrived(i):
        own_w[i].wait()
        arrive(w_slot(i, sibling), w_recv.at[i, sibling, 0])
        for k in range(1, X):
            s = flip(x, k) * 2 + 1 - c
            for j in range(4):
                arrive(w_part(i, s, j), w_recv.at[i, s, j])

    forward_weight(0)
    for k in range(1, A):
        if k == A - 1:
            forward_weight(1, end)
        for f in range(2):
            forward(ng[0][f], k, True)
    for f in range(2):
        hop(ng[0][f])
    for f in range(2):
        along(ng[1][f], mid)
    forward_weight(1, mid)
    weight_arrived(0)
    weight_arrived(1)

    H = A // 2
    pair = a // 2
    order = [*range(H - 1, 0, -1), 0]
    M = 4 * T2
    wide = 256 if Dq % 256 == 0 else Dq

    def g_rows(hh, g):
        return pl.ds(pl.multiple_of((hh * n + 4 * nearest(pair, H, order[g])) * T2, M), M)

    def gated(hh, g):
        rows = g_rows(hh, g)

        def step(j, carry):
            cols = pl.ds(pl.multiple_of(j * 256, 256), 256)
            gate = jnp.dot(nrm[rows, :], wgs[:, cols], preferred_element_type=f32)
            upper = jnp.dot(nrm[rows, :], wus[:, cols], preferred_element_type=f32)
            hid[g, :, cols] = (gate / (1.0 + jnp.exp(-gate)) * upper).astype(bf16)
            return carry

        lax.fori_loop(0, F // 256, step, 0, unroll=2)

    pieces = [flip(x, k) * 2 + cc for k in range(X) for cc in range(2)]

    def p_cols(p):
        return pl.ds(pl.multiple_of(pieces[p] * Dq, 128), Dq)

    def lowered(hh, g, p):
        rows = g_rows(hh, g)
        for i in range(Dq // wide):
            piece = jnp.dot(
                hid[g], wds[pieces[p], :, i * wide : (i + 1) * wide], preferred_element_type=f32
            )
            cols = pl.ds(pl.multiple_of(pieces[p] * Dq + i * wide, 128), wide)
            big[rows, cols] = piece.astype(bf16)

    def b_rows(hh, pos, plane):
        return n_rows(hh, pos * 2 + plane)

    def r_rows(hh, i):
        return pl.ds(pl.multiple_of((i * 2 + hh) * T2, T2), T2)

    def targets(g):
        there = nearest(pair, H, order[g])
        right = at_least(there, pair)
        return right, [2 * there + right, 2 * there + 1 - right]

    def y_at(hh, p, d):
        return yr.at[r_rows(hh, d), p_cols(p)], y_recv.at[hh * len(pieces) + p, d]

    def z_at(hh, p, i):
        return zr.at[r_rows(hh, i), p_cols(p)], z_recv.at[hh * len(pieces) + p, i]

    def cross(hh, p, d):
        dst, sem = y_at(hh, p, d)
        send(big.at[b_rows(hh, d, 1 - b), p_cols(p)], dst, sem, "mlp", partner)

    def add(rows, cols, *terms):
        total = big[rows, cols].astype(f32)
        for term in terms:
            total = total + term[...].astype(f32)
        big[rows, cols] = total.astype(bf16)

    def fed(d):
        return ((d > a) & has_l) | ((d < a) & has_r)

    def out(hh, p, d):
        src = big.at[b_rows(hh, d, 1 - b), p_cols(p)]
        right = at_least(d, a)
        dst, sem = z_at(hh, p, A + 2 - right)
        send(src, dst, sem, "mlp", (a + 2 * right - 1) * 2 + b, hopped(d))
        dst, sem = y_at(hh, p, d)
        send(src, dst, sem, "mlp", partner, jnp.logical_not(hopped(d)))

    def onward(hh, p, d, when=True):
        rows, cols = b_rows(hh, d, b), p_cols(p)
        right = at_least(d, a)
        z, zsem = z_at(hh, p, d)
        y, ysem = y_at(hh, p, d)
        zin, yin = fed(d) & when, jnp.logical_not(hopped(d)) & when
        arrive(z, zsem, zin)
        arrive(y, ysem, yin)
        pl.when(yin & zin)(lambda: add(rows, cols, y, z))
        pl.when(yin & jnp.logical_not(zin))(lambda: add(rows, cols, y))
        pl.when(zin & jnp.logical_not(yin))(lambda: add(rows, cols, z))
        to = a + 2 * right - 1
        into = d + (1 - right) * at_least(d, to) * (A - d)
        dst, sem = z_at(hh, p, into)
        send(big.at[rows, cols], dst, sem, "mlp", to * 2 + b, None if when is True else when)

    def far_out(hh, g, p):
        lowered(hh, g, p)
        for d in targets(g)[1]:
            out(hh, p, d)

    def far_on(hh, g, p, when=True):
        for d in targets(g)[1]:
            onward(hh, p, d, when)

    free = jnp.logical_not(fed(mate)) & hopped(mate)

    def near_out(hh, p):
        lowered(hh, H - 1, p)
        out(hh, p, mate)
        onward(hh, p, mate, free)

    def mate_on(hh, p):
        onward(hh, p, mate, jnp.logical_not(free))

    def own_on(hh, p):
        for d, i in ((a - 1, A + 1), (a + 1, A + 2)):
            z, zsem = z_at(hh, p, i)
            met = (d >= 0) & (d < A) & mid
            arrive(z, zsem, met)
            pl.when(met)(lambda z=z: add(b_rows(hh, a, 1 - b), p_cols(p), z))
        cross(hh, p, a)

    outs = []

    def finish(hh, p):
        rows, cols = pl.ds(hh * T2, T2), p_cols(p)
        y, ysem = y_at(hh, p, a)
        zl, lsem = z_at(hh, p, a)
        zr_, rsem = z_at(hh, p, A)
        arrive(y, ysem)
        total = h[rows, cols] + (big[b_rows(hh, a, b), cols].astype(f32) + y[...].astype(f32))
        h[rows, cols] = total
        for z, sem, met in ((zl, lsem, has_l), (zr_, rsem, has_r)):
            arrive(z, sem, met)

            def plus(z=z):
                h[rows, cols] = h[rows, cols] + z[...].astype(f32)

            pl.when(met)(plus)
        out_ref[rows, cols] = h[rows, cols].astype(bf16)
        copy = pltpu.make_async_copy(out_ref.at[rows, cols], out_hbm.at[rows, cols], out_sem.at[hh, p])
        copy.start()
        outs.append(copy)

    def down_forward(p):
        s = pieces[p]
        arrive(d_part(s, c), d_recv.at[s, c])
        send(d_part(s, c), d_part(s, c), d_recv.at[s, c], "req", sibling)

    def down_arrived(p):
        s = pieces[p]
        arrive(d_part(s, 1 - c), d_recv.at[s, 1 - c])

    def pass_on(k, when=True):
        for f in range(2):
            forward(ng[1][f], k, True, when)

    count = len(pieces)
    far = range(H - 1)

    def others(hh, g):
        there = nearest(pair, H, order[g])
        for f in range(2):
            if g < H - 1:
                other(ng[hh][f], 2 * there)
                other(ng[hh][f], 2 * there + 1)
            else:
                other(ng[hh][f], mate)

    others(0, H - 1)
    gated(0, H - 1)
    for p in range(2):
        near_out(0, p)
    for k in range(1, A - 1):
        pass_on(k, mid)
    for g in far:
        others(0, g)
        gated(0, g)
        for p in range(2):
            far_out(0, g, p)
    pass_on(1, end)
    down_forward(2)
    for p in range(2):
        own_on(0, p)
    pass_on(A - 1, mid)
    for f in range(2):
        hop(ng[1][f])
    for p in range(2):
        for g in far:
            far_on(0, g, p)
        mate_on(0, p)
    for k in range(2, A - 1):
        pass_on(k, end)

    def both_out(p):
        down_arrived(p)
        near_out(0, p)
        for g in far:
            far_out(0, g, p)

    both_out(2)
    pass_on(A - 1, end)
    for p in range(3, count):
        down_forward(p)
    for p in range(3, count):
        both_out(p)
    own_on(0, 2)
    for g in far:
        far_on(0, g, 2)
    others(1, H - 1)
    gated(1, H - 1)
    for p in range(2):
        near_out(1, p)
    for p in range(3, count):
        own_on(0, p)
        for g in far:
            far_on(0, g, p, end)
    for g in far:
        others(1, g)
        gated(1, g)
        for p in range(2):
            far_out(1, g, p)
    for p in range(3, count):
        for g in far:
            far_on(0, g, p, mid)
    for p in range(2, count):
        for g in far:
            far_out(1, g, p)
        near_out(1, p)
    for p in range(2, count):
        mate_on(0, p)
    for p in range(count + 1):
        if p < count:
            own_on(1, p)
            for g in far:
                far_on(1, g, p)
        if p > 0:
            mate_on(1, p - 1)
    for hh in range(2):
        for p in range(count):
            finish(hh, p)
    for copy in outs:
        copy.wait()
    for copy, when in slow + started[-ring:]:
        sent(copy, when)


def body(
    n, nr,
    resid, queries, fresh_keys, fresh_values, paged_key_cache, paged_value_cache,
    page_table, cache_lengths, out_weight, norm_gain, gate_weight, up_weight, down_weight,
):
    T, D = resid.shape
    own_pages, page_tokens = paged_key_cache.shape[:2]
    R = own_pages * page_tokens + T
    A, X = n // 2, nr // 2
    depth, F = gate_weight.shape
    Dq = down_weight.shape[1]
    pieces = nr
    sends = 96
    bf16, f32 = jnp.bfloat16, jnp.float32
    dma = pltpu.SemaphoreType.DMA
    vmem = pl.BlockSpec(memory_space=pltpu.VMEM)
    smem = pl.BlockSpec(memory_space=pltpu.SMEM)
    hbm = pl.BlockSpec(memory_space=pl.ANY)
    return pl.pallas_call(
        functools.partial(kernel, n, nr),
        out_shape=jax.ShapeDtypeStruct((T, D), bf16),
        in_specs=[smem] * 2 + [vmem] + [hbm] * 10,
        out_specs=hbm,
        scratch_shapes=[
            pltpu.VMEM((T, ATTN), bf16),
            pltpu.VMEM((T, D), bf16),
            pltpu.VMEM((T, D), bf16),
            pltpu.VMEM((n * R, KV_COLS), bf16),
            pltpu.VMEM((n * R, KV_COLS), bf16),
            pltpu.VMEM((n * T, D), bf16),
            pltpu.VMEM((nr * depth, F), bf16),
            pltpu.VMEM((nr * depth, F), bf16),
            pltpu.VMEM((nr, F, Dq), bf16),
            pltpu.VMEM((max(n * T, out_weight.shape[0]), D), bf16),
            pltpu.VMEM((A * T, D), bf16),
            pltpu.VMEM(((A + 3) * T, D), bf16),
            pltpu.VMEM((T, D), f32),
            pltpu.VMEM((T, ATTN), bf16),
            pltpu.VMEM((QUERY_HEADS // 2, 2 * T, 1), f32),
            pltpu.VMEM((QUERY_HEADS // 2, 2 * T, 1), f32),
            pltpu.VMEM((T, 2 * R), f32),
            pltpu.VMEM((A // 2, 2 * T, F), bf16),
            dma((4, max(own_pages + 1, 3))),
            dma((sends,)),
            dma((X, 10)),
            dma((2, n)),
            dma((4, n)),
            dma((3, nr, 4)),
            dma((nr, 2)),
            dma((2 * pieces, A)),
            dma((2 * pieces, A + 3)),
            dma((2, pieces)),
        ],
        compiler_params=pltpu.CompilerParams(
            collective_id=0, has_side_effects=True, vmem_limit_bytes=62 * 2**20
        ),
    )(
        page_table, cache_lengths, norm_gain.reshape(1, D), queries, resid, fresh_keys, fresh_values,
        paged_key_cache, paged_value_cache, out_weight, gate_weight, up_weight, down_weight,
    )


def solution(mesh):
    placed = (
        P(("req", "mlp"), None),
        P(("req", "mlp"), None),
        P(("req", "mlp"), None),
        P(("req", "mlp"), None),
        P(("req", "mlp"), None, None),
        P(("req", "mlp"), None, None),
        P("req", None),
        P("req"),
        P(),
        P(),
        P("req", "mlp"),
        P("req", "mlp"),
        P("mlp", "req"),
    )
    return jax.shard_map(
        functools.partial(body, mesh.shape["mlp"], mesh.shape["req"]),
        mesh=mesh, in_specs=placed, out_specs=P(("req", "mlp"), None), check_vma=False,
    )
```

```python
import functools
import math

import jax
import jax.numpy as jnp
from jax import lax
from jax.experimental import pallas as pl
from jax.experimental.pallas import tpu as pltpu
from jax.sharding import PartitionSpec as P

QUERY_HEADS = 12
KEY_VALUE_HEADS = 2
HEAD_SIZE = 128
GROUP = QUERY_HEADS // KEY_VALUE_HEADS
KV_COLS = KEY_VALUE_HEADS * HEAD_SIZE
ATTN = QUERY_HEADS * HEAD_SIZE
MESH = pl.DeviceIdType.MESH


def flip(a, k):
    bit = 1
    while bit <= k:
        if k & bit:
            a = a + bit - 2 * bit * (lax.rem(a // bit, 2))
        bit *= 2
    return a


def at_least(u, v):
    return (u - v + 1024) // 1024


def nearest(a, count, j):
    if j == 0:
        return a
    low = 1 - at_least(a, count // 2)
    room = low * a + (1 - low) * (count - 1 - a)
    both = at_least(2 * room, j)
    step = (j + 1) // 2
    return a + both * (-step if j % 2 else step) + (1 - both) * (2 * low - 1) * (j - room)


def kernel(
    n, nr,
    table, length, gain_ref, q_hbm, resid_hbm, fk, fv, pk, pv, ow, wg, wu, wd,
    out_hbm,
    q_ref, resid_ref, out_ref, kb, vb, nrm, wgs, wus, wds, big, yr, zr, h, attn, top, den, bias, hid,
    loc, ss, sx, kv_recv, n_recv, w_recv, d_recv, y_recv, z_recv, out_sem,
):
    A, X = n // 2, nr // 2
    me, r = lax.axis_index("mlp"), lax.axis_index("req")
    a, b = me // 2, lax.rem(me, 2)
    x, c = r // 2, lax.rem(r, 2)
    partner, sibling = a * 2 + 1 - b, x * 2 + 1 - c
    mate = a + 1 - 2 * lax.rem(a, 2)
    has_l, has_r = a > 0, a < A - 1
    T, D = resid_ref.shape
    T2 = T // 2
    own_pages, page_tokens = pk.shape[:2]
    cached = own_pages * page_tokens
    R = cached + T
    depth, F = wg.shape
    Dq = wd.shape[1]
    bf16, f32 = jnp.bfloat16, jnp.float32

    def rpeer(k):
        return flip(x, k) * 2 + c

    def remote(src, dst, sem, recv_sem, axis, idx):
        return pltpu.make_async_remote_copy(
            src_ref=src, dst_ref=dst, send_sem=sem, recv_sem=recv_sem,
            device_id={axis: idx}, device_id_type=MESH,
        )

    ring = ss.shape[0]
    started, slow = [], []

    def sent(copy, when):
        if when is None:
            copy.wait_send()
        else:
            pl.when(when)(copy.wait_send)

    def send(src, dst, recv_sem, axis, idx, when=None, sem=None):
        if sem is None:
            if len(started) >= ring:
                sent(*started[-ring])
            sem = ss.at[len(started) % ring]
            kept = started
        else:
            kept = slow
        copy = remote(src, dst, sem, recv_sem, axis, idx)
        kept.append((copy, when))
        if when is None:
            copy.start()
        else:
            pl.when(when)(copy.start)

    def arrive(ref, recv_sem, when=None):
        copy = remote(ref, ref, recv_sem, recv_sem, "mlp", partner)
        if when is None:
            copy.wait_recv()
        else:
            pl.when(when)(copy.wait_recv)

    base = pl.multiple_of(me * R, 128)
    mine = []
    for i, (buf, pages, fresh) in enumerate(((kb, pk, fk), (vb, pv, fv))):
        for j in range(own_pages):
            mine.append(pltpu.make_async_copy(
                pages.at[j], buf.at[pl.ds(base + j * page_tokens, page_tokens), :], loc.at[i, j]))
        mine.append(pltpu.make_async_copy(fresh, buf.at[pl.ds(base + cached, T), :], loc.at[i, own_pages]))
    for copy in mine:
        copy.start()

    def w_slot(i, s):
        if i == 2:
            return wds.at[s]
        buf = wgs if i == 0 else wus
        return buf.at[pl.ds(pl.multiple_of(s * depth, 128), depth), :]

    quarter = depth // 4

    def w_part(i, s, j):
        buf = wgs if i == 0 else wus
        return buf.at[pl.ds(pl.multiple_of(s * depth + j * quarter, 16), quarter), :]

    weights = (wg, wu, wd)
    own_w = [pltpu.make_async_copy(weights[i], w_slot(i, r), loc.at[2, i]) for i in range(3)]
    own_q = pltpu.make_async_copy(q_hbm, q_ref, loc.at[3, 1])
    own_resid = pltpu.make_async_copy(resid_hbm, resid_ref, loc.at[3, 2])
    own_ow = pltpu.make_async_copy(ow, big.at[pl.ds(0, ATTN), :], loc.at[3, 0])

    own_q.start()
    own_resid.start()
    barrier = pltpu.get_barrier_semaphore()

    def greet(axis, idx):
        pl.semaphore_signal(barrier, inc=1, device_id={axis: idx}, device_id_type=MESH)

    greet("mlp", partner)
    greet("req", sibling)
    for k in range(1, X):
        greet("req", rpeer(k))
    pl.when(has_l)(lambda: greet("mlp", me - 2))
    pl.when(has_r)(lambda: greet("mlp", me + 2))
    pl.semaphore_wait(barrier, X + 1 + has_l.astype(jnp.int32) + has_r.astype(jnp.int32))

    def kv_slot(part):
        buf = (kb, vb)[part]
        return lambda s: buf.at[pl.ds(pl.multiple_of(s * R, 128), R), :], lambda s: kv_recv.at[part, s]

    half = D // 2

    def n_rows(hh, s):
        return pl.ds(pl.multiple_of((hh * n + s) * T2, T2), T2)

    def n_slot(hh, f):
        return (
            lambda s: nrm.at[n_rows(hh, s), pl.ds(f * half, half)],
            lambda s: n_recv.at[hh * 2 + f, s],
        )

    def along(kind, when=True):
        slot, sem = kind
        send(slot(me), slot(me), sem(me), "mlp", me + 2, has_r & when)
        send(slot(me), slot(me), sem(me), "mlp", me - 2, has_l & when)

    def across(kind):
        slot, sem = kind
        send(slot(me), slot(me), sem(me), "mlp", partner)

    def spread(kind):
        along(kind)
        across(kind)

    end = (a == 0) | (a == A - 1)
    mid = jnp.logical_not(end)

    def hopped(pos):
        return (pos <= a + 1) & (pos >= a - 1) & (pos != a) & (pos > 0) & (pos < A - 1)

    def forward(kind, k, hops, when=True):
        slot, sem = kind
        pos = nearest(a, A, k)
        s = pos * 2 + b
        arrive(slot(s), sem(s), None if when is True else when)
        right = at_least(a, pos)
        to = a + 2 * right - 1
        send(slot(s), slot(s), sem(s), "mlp", to * 2 + b, (to >= 0) & (to < A) & when)
        crosses = jnp.logical_not(hopped(pos)) & when if hops else (None if when is True else when)
        send(slot(s), slot(s), sem(s), "mlp", partner, crosses)

    def hop(kind):
        slot, sem = kind
        arrive(slot(partner), sem(partner))
        for to, there in ((a + 1, has_r), (a - 1, has_l)):
            send(slot(partner), slot(partner), sem(partner), "mlp", to * 2 + b, there & mid)

    def other(kind, pos):
        slot, sem = kind
        s = pos * 2 + 1 - b
        arrive(slot(s), sem(s))

    kv = [kv_slot(0), kv_slot(1)]
    for part in range(2):
        for copy in mine[part * (own_pages + 1) : (part + 1) * (own_pages + 1)]:
            copy.wait()
        spread(kv[part])
    for i in range(2):
        for k in range(1, X):
            for j in range(4):
                part = weights[i].at[pl.ds(j * quarter, quarter), :]
                send(part, w_part(i, r, j), w_recv.at[i, r, j], "req", rpeer(k), sem=sx.at[k, i * 4 + j])
    own_w[2].start()
    send(wd, w_slot(2, r), w_recv.at[2, r, 0], "req", sibling)
    own_ow.start()
    for i in range(2):
        own_w[i].start()
        send(weights[i], w_slot(i, r), w_recv.at[i, r, 0], "req", sibling)

    factor = HEAD_SIZE ** (-0.5) * math.log2(math.e)
    ahead = lax.broadcasted_iota(jnp.int32, (T, T), 1) - lax.broadcasted_iota(jnp.int32, (T, T), 0)
    lane = lax.broadcasted_iota(jnp.int32, (T, page_tokens), 1)

    def mask(pos):
        for j in range(2):
            s = pos * 2 + j
            for p in range(own_pages):
                page = jnp.int32(0)
                for i in range(table.shape[1]):
                    page = page + jnp.where(table[0, i] == s * own_pages + p, i, 0)
                live = lane < length[0] - page * page_tokens
                bias[:, j * R + p * page_tokens : j * R + (p + 1) * page_tokens] = jnp.where(live, 0.0, -1e30)
            bias[:, j * R + cached : (j + 1) * R] = jnp.where(ahead <= (me - s) * T, 0.0, -1e30)

    def attend(pos, last=False):
        rows = pl.ds(pl.multiple_of(pos * 2 * R, 128), 2 * R)

        def step(i, carry):
            head = 2 * i
            g = head // GROUP
            c0 = pl.ds(pl.multiple_of(head * HEAD_SIZE, 128), HEAD_SIZE)
            c1 = pl.ds(pl.multiple_of(head * HEAD_SIZE + HEAD_SIZE, 128), HEAD_SIZE)
            gc = pl.ds(pl.multiple_of(g * HEAD_SIZE, 128), HEAD_SIZE)
            qq = jnp.concatenate([q_ref[:, c0], q_ref[:, c1]], axis=0)
            s = lax.dot_general(
                qq, kb[rows, gc], (((1,), (1,)), ((), ())), preferred_element_type=f32
            )
            s = ((s * factor).reshape(2, T, 2 * R) + bias[...][None]).reshape(2 * T, 2 * R)
            before = top[i]
            most = jnp.maximum(jnp.max(s, axis=-1, keepdims=True), before)
            scale = jnp.exp2(before - most)
            e = jnp.exp2(s - most)
            total = jnp.sum(e, axis=-1, keepdims=True) + den[i] * scale
            o = jnp.dot(e.astype(bf16), vb[rows, gc], preferred_element_type=f32)
            o = o + jnp.concatenate([h[:, c0], h[:, c1]], axis=0) * scale
            if last:
                o = o / total
                attn[:, c0] = o[:T].astype(bf16)
                attn[:, c1] = o[T:].astype(bf16)
            else:
                top[i] = most
                den[i] = total
                h[:, c0] = o[:T]
                h[:, c1] = o[T:]
            return carry

        lax.fori_loop(0, QUERY_HEADS // 2, step, 0, unroll=2)

    def both(f, *args):
        for part in range(2):
            f(kv[part], *args)

    def stage(pos, last=False):
        mask(pos)
        both(other, pos)
        attend(pos, last)

    ended = 1 - at_least(a, 1) + at_least(a, A - 1)

    def turn(k):
        return ended * nearest(a, A, k - 1) + (1 - ended) * nearest(a, A, max(k - 2, 0))

    top[...] = jnp.full_like(top, -2e30)
    den[...] = jnp.zeros_like(den)
    h[...] = jnp.zeros_like(h)
    fh = F // 2

    def d_part(s, part):
        return wds.at[s, pl.ds(pl.multiple_of(part * fh, 16), fh), :]

    own_q.wait()
    own_resid.wait()
    for k in range(1, A):
        both(forward, k, False)
        if k == 1:
            pl.when(end)(lambda: stage(nearest(a, A, 0)))
            own_w[2].wait()
            arrive(w_slot(2, sibling), w_recv.at[2, sibling, 0])
            for cc in range(2):
                for kk in range(1, X):
                    s = x * 2 + cc
                    send(d_part(s, c), d_part(s, c), d_recv.at[s, c], "req", rpeer(kk), sem=sx.at[kk, 8 + cc])
        else:
            stage(turn(k))
    pl.when(mid)(lambda: stage(nearest(a, A, A - 2)))
    stage(nearest(a, A, A - 1), True)

    own_ow.wait()

    def project(j, squares):
        cols = pl.ds(pl.multiple_of(j * 256, 256), 256)
        piece = resid_ref[:, cols].astype(f32) + jnp.dot(
            attn[...], big[pl.ds(0, ATTN), cols], preferred_element_type=f32
        )
        h[:, cols] = piece
        return squares + jnp.sum(piece * piece, axis=-1, keepdims=True)

    squares = lax.fori_loop(0, D // 256, project, jnp.zeros((T, 1), f32), unroll=6)
    inverse = lax.rsqrt(squares / D + 1e-05)
    ng = [[n_slot(hh, f) for f in range(2)] for hh in range(2)]
    for hh in range(2):
        rows = pl.ds(hh * T2, T2)
        nrm[n_rows(hh, me), :] = (
            h[rows, :] * inverse[hh * T2 : (hh + 1) * T2] * gain_ref[...]
        ).astype(bf16)
        for f in range(2):
            if hh == 0:
                spread(ng[0][f])
            else:
                across(ng[1][f])
                along(ng[1][f], end)

    def forward_weight(i, when=None):
        for k in range(1, X):
            s = rpeer(k)
            for j in range(4):
                arrive(w_part(i, s, j), w_recv.at[i, s, j], when)
                send(w_part(i, s, j), w_part(i, s, j), w_recv.at[i, s, j], "req", sibling, when)

    def weight_arrived(i):
        own_w[i].wait()
        arrive(w_slot(i, sibling), w_recv.at[i, sibling, 0])
        for k in range(1, X):
            s = flip(x, k) * 2 + 1 - c
            for j in range(4):
                arrive(w_part(i, s, j), w_recv.at[i, s, j])

    forward_weight(0)
    for k in range(1, A):
        if k == A - 1:
            forward_weight(1, end)
        for f in range(2):
            forward(ng[0][f], k, True)
    for f in range(2):
        hop(ng[0][f])
    for f in range(2):
        along(ng[1][f], mid)
    forward_weight(1, mid)
    weight_arrived(0)
    weight_arrived(1)

    H = A // 2
    pair = a // 2
    order = [*range(H - 1, 0, -1), 0]
    M = 4 * T2
    wide = 256 if Dq % 256 == 0 else Dq

    def g_rows(hh, g):
        return pl.ds(pl.multiple_of((hh * n + 4 * nearest(pair, H, order[g])) * T2, M), M)

    def gated(hh, g):
        rows = g_rows(hh, g)

        def step(j, carry):
            cols = pl.ds(pl.multiple_of(j * 256, 256), 256)
            gate = jnp.dot(nrm[rows, :], wgs[:, cols], preferred_element_type=f32)
            upper = jnp.dot(nrm[rows, :], wus[:, cols], preferred_element_type=f32)
            hid[g, :, cols] = (gate / (1.0 + jnp.exp(-gate)) * upper).astype(bf16)
            return carry

        lax.fori_loop(0, F // 256, step, 0, unroll=2)

    pieces = [flip(x, k) * 2 + cc for k in range(X) for cc in range(2)]

    def p_cols(p):
        return pl.ds(pl.multiple_of(pieces[p] * Dq, 128), Dq)

    def lowered(hh, g, p):
        rows = g_rows(hh, g)
        for i in range(Dq // wide):
            piece = jnp.dot(
                hid[g], wds[pieces[p], :, i * wide : (i + 1) * wide], preferred_element_type=f32
            )
            cols = pl.ds(pl.multiple_of(pieces[p] * Dq + i * wide, 128), wide)
            big[rows, cols] = piece.astype(bf16)

    def b_rows(hh, pos, plane):
        return n_rows(hh, pos * 2 + plane)

    def r_rows(hh, i):
        return pl.ds(pl.multiple_of((i * 2 + hh) * T2, T2), T2)

    def targets(g):
        there = nearest(pair, H, order[g])
        right = at_least(there, pair)
        return right, [2 * there + right, 2 * there + 1 - right]

    def y_at(hh, p, d):
        return yr.at[r_rows(hh, d), p_cols(p)], y_recv.at[hh * len(pieces) + p, d]

    def z_at(hh, p, i):
        return zr.at[r_rows(hh, i), p_cols(p)], z_recv.at[hh * len(pieces) + p, i]

    def cross(hh, p, d):
        dst, sem = y_at(hh, p, d)
        send(big.at[b_rows(hh, d, 1 - b), p_cols(p)], dst, sem, "mlp", partner)

    def add(rows, cols, *terms):
        total = big[rows, cols].astype(f32)
        for term in terms:
            total = total + term[...].astype(f32)
        big[rows, cols] = total.astype(bf16)

    def fed(d):
        return ((d > a) & has_l) | ((d < a) & has_r)

    def out(hh, p, d):
        src = big.at[b_rows(hh, d, 1 - b), p_cols(p)]
        right = at_least(d, a)
        dst, sem = z_at(hh, p, A + 2 - right)
        send(src, dst, sem, "mlp", (a + 2 * right - 1) * 2 + b, hopped(d))
        dst, sem = y_at(hh, p, d)
        send(src, dst, sem, "mlp", partner, jnp.logical_not(hopped(d)))

    def onward(hh, p, d, when=True):
        rows, cols = b_rows(hh, d, b), p_cols(p)
        right = at_least(d, a)
        z, zsem = z_at(hh, p, d)
        y, ysem = y_at(hh, p, d)
        zin, yin = fed(d) & when, jnp.logical_not(hopped(d)) & when
        arrive(z, zsem, zin)
        arrive(y, ysem, yin)
        pl.when(yin & zin)(lambda: add(rows, cols, y, z))
        pl.when(yin & jnp.logical_not(zin))(lambda: add(rows, cols, y))
        pl.when(zin & jnp.logical_not(yin))(lambda: add(rows, cols, z))
        to = a + 2 * right - 1
        into = d + (1 - right) * at_least(d, to) * (A - d)
        dst, sem = z_at(hh, p, into)
        send(big.at[rows, cols], dst, sem, "mlp", to * 2 + b, None if when is True else when)

    def far_out(hh, g, p):
        lowered(hh, g, p)
        for d in targets(g)[1]:
            out(hh, p, d)

    def far_on(hh, g, p, when=True):
        for d in targets(g)[1]:
            onward(hh, p, d, when)

    free = jnp.logical_not(fed(mate)) & hopped(mate)

    def near_out(hh, p):
        lowered(hh, H - 1, p)
        out(hh, p, mate)
        onward(hh, p, mate, free)

    def mate_on(hh, p):
        onward(hh, p, mate, jnp.logical_not(free))

    def own_on(hh, p):
        for d, i in ((a - 1, A + 1), (a + 1, A + 2)):
            z, zsem = z_at(hh, p, i)
            met = (d >= 0) & (d < A) & mid
            arrive(z, zsem, met)
            pl.when(met)(lambda z=z: add(b_rows(hh, a, 1 - b), p_cols(p), z))
        cross(hh, p, a)

    outs = []

    def finish(hh, p):
        rows, cols = pl.ds(hh * T2, T2), p_cols(p)
        y, ysem = y_at(hh, p, a)
        zl, lsem = z_at(hh, p, a)
        zr_, rsem = z_at(hh, p, A)
        arrive(y, ysem)
        total = h[rows, cols] + (big[b_rows(hh, a, b), cols].astype(f32) + y[...].astype(f32))
        h[rows, cols] = total
        for z, sem, met in ((zl, lsem, has_l), (zr_, rsem, has_r)):
            arrive(z, sem, met)

            def plus(z=z):
                h[rows, cols] = h[rows, cols] + z[...].astype(f32)

            pl.when(met)(plus)
        out_ref[rows, cols] = h[rows, cols].astype(bf16)
        copy = pltpu.make_async_copy(out_ref.at[rows, cols], out_hbm.at[rows, cols], out_sem.at[hh, p])
        copy.start()
        outs.append(copy)

    def down_forward(p):
        s = pieces[p]
        arrive(d_part(s, c), d_recv.at[s, c])
        send(d_part(s, c), d_part(s, c), d_recv.at[s, c], "req", sibling)

    def down_arrived(p):
        s = pieces[p]
        arrive(d_part(s, 1 - c), d_recv.at[s, 1 - c])

    def pass_on(k, when=True):
        for f in range(2):
            forward(ng[1][f], k, True, when)

    count = len(pieces)
    far = range(H - 1)

    def others(hh, g):
        there = nearest(pair, H, order[g])
        for f in range(2):
            if g < H - 1:
                other(ng[hh][f], 2 * there)
                other(ng[hh][f], 2 * there + 1)
            else:
                other(ng[hh][f], mate)

    others(0, H - 1)
    gated(0, H - 1)
    for p in range(2):
        near_out(0, p)
    for k in range(1, A - 1):
        pass_on(k, mid)
    for g in far:
        others(0, g)
        gated(0, g)
        for p in range(2):
            far_out(0, g, p)
    pass_on(1, end)
    down_forward(2)
    for p in range(2):
        own_on(0, p)
    pass_on(A - 1, mid)
    for f in range(2):
        hop(ng[1][f])
    for p in range(2):
        for g in far:
            far_on(0, g, p)
        mate_on(0, p)
    for k in range(2, A - 1):
        pass_on(k, end)

    def both_out(p):
        down_arrived(p)
        near_out(0, p)
        for g in far:
            far_out(0, g, p)

    both_out(2)
    pass_on(A - 1, end)
    for p in range(3, count):
        down_forward(p)
    for p in range(3, count):
        both_out(p)
    own_on(0, 2)
    for g in far:
        far_on(0, g, 2)
    others(1, H - 1)
    gated(1, H - 1)
    for p in range(2):
        near_out(1, p)
    for p in range(3, count):
        own_on(0, p)
        for g in far:
            far_on(0, g, p, end)
    for g in far:
        others(1, g)
        gated(1, g)
        for p in range(2):
            far_out(1, g, p)
    for p in range(3, count):
        for g in far:
            far_on(0, g, p, mid)
    for p in range(2, count):
        for g in far:
            far_out(1, g, p)
        near_out(1, p)
    for p in range(2, count):
        mate_on(0, p)
    for p in range(count + 1):
        if p < count:
            own_on(1, p)
            for g in far:
                far_on(1, g, p)
        if p > 0:
            mate_on(1, p - 1)
    for hh in range(2):
        for p in range(count):
            finish(hh, p)
    for copy in outs:
        copy.wait()
    for copy, when in slow + started[-ring:]:
        sent(copy, when)


def body(
    n, nr,
    resid, queries, fresh_keys, fresh_values, paged_key_cache, paged_value_cache,
    page_table, cache_lengths, out_weight, norm_gain, gate_weight, up_weight, down_weight,
):
    T, D = resid.shape
    own_pages, page_tokens = paged_key_cache.shape[:2]
    R = own_pages * page_tokens + T
    A, X = n // 2, nr // 2
    depth, F = gate_weight.shape
    Dq = down_weight.shape[1]
    pieces = nr
    sends = 80
    bf16, f32 = jnp.bfloat16, jnp.float32
    dma = pltpu.SemaphoreType.DMA
    vmem = pl.BlockSpec(memory_space=pltpu.VMEM)
    smem = pl.BlockSpec(memory_space=pltpu.SMEM)
    hbm = pl.BlockSpec(memory_space=pl.ANY)
    return pl.pallas_call(
        functools.partial(kernel, n, nr),
        out_shape=jax.ShapeDtypeStruct((T, D), bf16),
        in_specs=[smem] * 2 + [vmem] + [hbm] * 10,
        out_specs=hbm,
        scratch_shapes=[
            pltpu.VMEM((T, ATTN), bf16),
            pltpu.VMEM((T, D), bf16),
            pltpu.VMEM((T, D), bf16),
            pltpu.VMEM((n * R, KV_COLS), bf16),
            pltpu.VMEM((n * R, KV_COLS), bf16),
            pltpu.VMEM((n * T, D), bf16),
            pltpu.VMEM((nr * depth, F), bf16),
            pltpu.VMEM((nr * depth, F), bf16),
            pltpu.VMEM((nr, F, Dq), bf16),
            pltpu.VMEM((max(n * T, out_weight.shape[0]), D), bf16),
            pltpu.VMEM((A * T, D), bf16),
            pltpu.VMEM(((A + 3) * T, D), bf16),
            pltpu.VMEM((T, D), f32),
            pltpu.VMEM((T, ATTN), bf16),
            pltpu.VMEM((QUERY_HEADS // 2, 2 * T, 1), f32),
            pltpu.VMEM((QUERY_HEADS // 2, 2 * T, 1), f32),
            pltpu.VMEM((T, 2 * R), f32),
            pltpu.VMEM((A // 2, 2 * T, F), bf16),
            dma((4, max(own_pages + 1, 3))),
            dma((sends,)),
            dma((X, 10)),
            dma((2, n)),
            dma((4, n)),
            dma((3, nr, 4)),
            dma((nr, 2)),
            dma((2 * pieces, A)),
            dma((2 * pieces, A + 3)),
            dma((2, pieces)),
        ],
        compiler_params=pltpu.CompilerParams(
            collective_id=0, has_side_effects=True, vmem_limit_bytes=62 * 2**20
        ),
    )(
        page_table, cache_lengths, norm_gain.reshape(1, D), queries, resid, fresh_keys, fresh_values,
        paged_key_cache, paged_value_cache, out_weight, gate_weight, up_weight, down_weight,
    )


def solution(mesh):
    placed = (
        P(("req", "mlp"), None),
        P(("req", "mlp"), None),
        P(("req", "mlp"), None),
        P(("req", "mlp"), None),
        P(("req", "mlp"), None, None),
        P(("req", "mlp"), None, None),
        P("req", None),
        P("req"),
        P(),
        P(),
        P("req", "mlp"),
        P("req", "mlp"),
        P("mlp", "req"),
    )
    return jax.shard_map(
        functools.partial(body, mesh.shape["mlp"], mesh.shape["req"]),
        mesh=mesh, in_specs=placed, out_specs=P(("req", "mlp"), None), check_vma=False,
    )
```
